32 devices in a mesh: grp: 2 (over y), sub: 16 (over z, x, core).
Axes of the slice: x: 2, y: 2, z: 4, core: 2. Of those that a mesh axis runs over, the one named last changes fastest.
Arguments:
- factors: bfloat16 [96, 1024, 1024], P(('grp', 'sub')), parts along dimension 0, may hold values from -0.1875 to 0.1875
- coupling: bfloat16 [96, 1024, 512], P(('grp', 'sub')), parts along dimension 0, may hold values from -0.1875 to 0.1875
- gap_loads: bfloat16 [96, 512, 256], P(('grp', 'sub')), parts along dimension 0, may hold values from -6 to 6
- dof_blocks: int32 [96], P(('grp', 'sub')), parts along dimension 0, may hold values from 4 to 8, as said below
- partner_rows: int32 [96, 512], P(('grp', 'sub')), parts along dimension 0, may hold values from 0 to 24575, as said below
Outputs:
- multipliers: float32 [96, 512, 256], P(('grp', 'sub')), parts along dimension 0
- dual_residual: float32 [96, 512, 256], P(('grp', 'sub')), parts along dimension 0
- residual_rms: float32 [512], P('grp'), parts along dimension 0
The draws below stay inside these ranges and needn't reach their ends.
There are 2 independent parts, one for each index of `grp`. The reference program is written for one: setup_inputs(seed, part) draws one part's arguments, and reference() takes and returns one part's arrays. A program takes and returns all parts, laid end to end along the dimension named above; each array names one. Nothing has to cross between parts.
Inputs may be any that keep to these rules, and one draw needn't show every extreme that they name: `partner_rows`: every interface row is tied to exactly one row of a subdomain on another device, and that row is tied back to it. The rows of one device are tied to at most 112 rows of any one other device, and some pair of devices reaches that number in every draw. `dof_blocks`: some subdomain has all 1024 degrees of freedom present in every draw.
All inputs are finite; a program needn't handle non-finite values.
Results may differ from the reference program's by a relative error of at most 0.008.
Values may be sent and summed in bfloat16 or wider, within the bound.
A program may use at most 64 MiB of HBM per device.

```python
import jax
import jax.numpy as jnp
from jax import lax

NDOF = 1024
IF = 512
DBLK = 128
FROWS = 16
NRHS = 256
ITERS = 3
SUB_DEV = 3
SUBS = 48
N_SUB = 16


def draw_gap_loads(key, part):
    subdomains = SUB_DEV * N_SUB
    first_key = jax.random.fold_in(key, 0)
    rising = (jnp.arange(subdomains, dtype=jnp.float32) / subdomains)[:, None, None]
    values = jnp.clip(jax.random.normal(first_key, (subdomains, IF, NRHS), jnp.float32), -4.0, 4.0) * (0.5 + rising)
    return values.astype(jnp.bfloat16)


def draw_dof_blocks(key, part):
    subdomains = SUB_DEV * N_SUB
    lowest = IF // DBLK
    highest = NDOF // DBLK
    first_key, second_key, third_key = jax.random.split(key, 3)
    extra = jax.random.randint(first_key, (subdomains,), 0, highest - lowest + 1)
    heavy = jax.random.randint(second_key, (subdomains,), 0, 2)
    blocks = lowest + extra * heavy
    chosen = jax.random.randint(third_key, (), 0, subdomains)
    blocks = jnp.where(jnp.arange(subdomains) == chosen, highest, blocks)
    return blocks.astype(jnp.int32)


def draw_partner_rows(key, part):
    row_count = SUB_DEV * IF
    faces = row_count // FROWS
    spread = max(N_SUB // 2 - 1, 1)
    first_key, second_key, third_key = jax.random.split(key, 3)
    labels = jax.random.permutation(first_key, N_SUB).astype(jnp.int32)
    holders = jnp.argsort(labels).astype(jnp.int32)
    scores = jax.random.randint(second_key, (N_SUB, faces), 0, 1 << 20) * faces + jnp.arange(faces, dtype=jnp.int32)[None, :]
    shuffle = jnp.argsort(scores, axis=1).astype(jnp.int32)
    logical = jnp.arange(faces, dtype=jnp.int32)
    offsets = 1 + logical // 2 % spread
    upward = logical % 2 == 0
    moved = jnp.where(upward, offsets, -offsets)
    other_label = (labels[:, None] + moved[None, :]) % N_SUB
    others = holders[other_label]
    other_logical = logical + 1 - 2 * (logical % 2)
    other_face = shuffle[others, other_logical[None, :]]
    even_label = jnp.where(upward[None, :], labels[:, None], other_label)
    pair_index = even_label * (faces // 2) + logical[None, :] // 2
    turns = jax.random.randint(third_key, (N_SUB * (faces // 2),), 0, FROWS)[pair_index]
    within = jnp.arange(FROWS, dtype=jnp.int32)
    forward = (within[None, None, :] + turns[:, :, None]) % FROWS
    backward = (within[None, None, :] - turns[:, :, None]) % FROWS
    partner_within = jnp.where(upward[None, :, None], forward, backward)
    target = others[:, :, None] * row_count + other_face[:, :, None] * FROWS + partner_within
    inverse = jnp.argsort(shuffle, axis=1).astype(jnp.int32)
    placed = jnp.take_along_axis(target, inverse[:, :, None], axis=1)
    return placed.reshape(SUB_DEV * N_SUB, IF).astype(jnp.int32)


def shard_levels(own_key, extent, pieces, low, largest):
    loudness, own = 1.0, jax.random.fold_in(own_key, 6)
    for position, blocks in pieces:
        steps = jnp.exp(jax.random.uniform(jax.random.fold_in(own, position), (blocks,), jnp.float32, low / len(pieces), largest / len(pieces)))
        loudness = loudness * jnp.repeat(steps, extent[position] // blocks).reshape([-1 if axis == position else 1 for axis in range(len(extent))])
    return loudness


def scatter_about(stream_key, extent, width, reach, shards=(), held_as=jnp.bfloat16):
    entries = width * jax.random.normal(stream_key, extent, jnp.float32)
    if shards:
        entries = entries * shard_levels(stream_key, extent, shards, -0.22, 0.18)
    return jnp.clip(entries, -reach, reach).astype(held_as)


def setup_inputs(seed: int = 0, part: int = 0) -> dict:
    key_of = jax.random.split(jax.random.key(seed), 6)
    own_keys = jax.random.split(jax.random.fold_in(key_of[5], part), 6)
    factors = scatter_about(own_keys[0], (SUBS, NDOF, NDOF), NDOF ** -0.5, 0.1875, ((0, 16),))
    coupling = scatter_about(own_keys[1], (SUBS, NDOF, IF), NDOF ** -0.5, 0.1875, ((0, 16),))
    gap_loads = draw_gap_loads(jax.random.fold_in(jax.random.fold_in(key_of[5], part), 71), part)
    dof_blocks = draw_dof_blocks(jax.random.fold_in(jax.random.fold_in(key_of[5], part), 71), part)
    partner_rows = draw_partner_rows(jax.random.fold_in(jax.random.fold_in(key_of[5], part), 71), part)
    return dict(factors=factors, coupling=coupling, gap_loads=gap_loads, dof_blocks=dof_blocks, partner_rows=partner_rows)


STEP_SIZE = 0.25

def build_panel(inputs):
    factor, couple, blocks = inputs
    present = jnp.arange(factor.shape[0]) < blocks * DBLK
    masked = jnp.where(present[:, None], couple, jnp.zeros_like(couple))
    product = jnp.dot(factor.T, masked, preferred_element_type=jnp.float32)
    reduced = jnp.where(present[:, None], product, jnp.zeros_like(product)).astype(jnp.bfloat16)
    schur_panel = jnp.dot(reduced.T, reduced, preferred_element_type=jnp.float32)
    return schur_panel.astype(jnp.bfloat16)

def reference(factors, coupling, gap_loads, dof_blocks, partner_rows):
    panels = lax.map(build_panel, (factors, coupling, dof_blocks))
    subdomains, interface, load_cases = gap_loads.shape
    partners = partner_rows.reshape(-1).astype(jnp.int32)
    own_rows = jnp.arange(partners.shape[0], dtype=jnp.int32)
    orient = jnp.where(own_rows < partners, 1.0, -1.0).astype(jnp.float32).reshape(subdomains, interface, 1)
    load_values = gap_loads.astype(jnp.float32)

    def pair_add(values):
        flat_values = values.reshape(-1, load_cases)
        return (flat_values + flat_values[partners]).reshape(values.shape)
    residual = pair_add(orient * load_values)
    multipliers = jnp.zeros_like(residual)
    for iteration in range(ITERS):
        multipliers = multipliers + STEP_SIZE * residual
        signed = (orient * multipliers).astype(jnp.bfloat16)
        panel_image = jnp.einsum('sij,sjc->sic', panels.astype(jnp.float32), signed.astype(jnp.float32), precision=lax.Precision.HIGHEST)
        residual = pair_add(orient * (load_values - panel_image))
    squares = lax.optimization_barrier(jnp.mean(residual * residual, axis=(0, 1)))
    return (multipliers, residual, jnp.sqrt(squares + 1e-06))
```

```python
import functools

import jax
import jax.numpy as jnp
from jax import lax
from jax.experimental import pallas as pl
from jax.experimental.pallas import tpu as pltpu
from jax.sharding import PartitionSpec as P

DBLK = 128
FROWS = 16
ITERS = 3
STEP_SIZE = 0.25
LANES = 128
F32 = jnp.float32
BF16 = jnp.bfloat16


def flipped(me, distance, devices):
    peer = 0
    bit = 1
    while bit < devices:
        peer = peer + bit * ((me // bit + distance // bit) % 2)
        bit *= 2
    return peer


def kernel(
    devices, capacity, blocks_ref, factors, coupling, gap_loads, partners,
    mult_out, resid_out, rms_out,
    gap, fac, cou, pack, pick, panel, turned, reduced, send, recv, low, term, mu, sign,
    key, sq_send, sq_recv,
    gap_sem, fac_sem, cou_sem, send_sem, recv_sem, sqs_sem, sqr_sem,
):
    subs, rows, cases = gap.shape
    dof = factors.shape[1]
    count = subs * rows
    halves = cases // LANES
    slots = devices * capacity
    wide = pick.shape[1]
    me = lax.axis_index("sub")
    parts = min(4, devices)
    group = devices // parts
    piece = slots // parts
    part = me // group
    inner = [flipped(me % group, d, group) for d in range(group)]

    def each_peer(far, action):
        side = flipped(part, far, parts)
        for d in range(group):
            peer = side * group + inner[d]
            if d > 0:
                action(peer)
            else:
                pl.when(far > 0)(functools.partial(action, peer))

    def fac_copy(s):
        return pltpu.make_async_copy(factors.at[s], fac.at[s], fac_sem.at[s])

    def cou_copy(s):
        return pltpu.make_async_copy(coupling.at[s], cou.at[s], cou_sem.at[s])

    gap_copy = pltpu.make_async_copy(gap_loads, gap, gap_sem)
    gap_copy.start()
    for s in range(subs):
        cou_copy(s).start()
        fac_copy(s).start()

    barrier = pltpu.get_barrier_semaphore()

    @pl.loop(0, parts)
    def _(i):
        def greet(peer):
            pl.semaphore_signal(
                barrier, inc=1, device_id={"sub": peer}, device_id_type=pl.DeviceIdType.MESH
            )

        each_peer(parts - 1 - i, greet)

    for e in range(recv.shape[0]):
        recv[e, pl.ds(pl.multiple_of(me * capacity, capacity), capacity), :] = jnp.zeros((capacity, LANES), BF16)
        if wide > slots:
            recv[e, slots:, :] = jnp.zeros((wide - slots, LANES), BF16)

    partner_row = jnp.concatenate([partners[s : s + 1, :] for s in range(subs)], axis=1).astype(F32)
    target_row = jnp.floor((partner_row + 0.5) * (1.0 / count))
    upper = (
        lax.broadcasted_iota(jnp.int32, (LANES, LANES), 0)
        <= lax.broadcasted_iota(jnp.int32, (LANES, LANES), 1)
    ).astype(F32).astype(BF16)
    peers = lax.broadcasted_iota(jnp.int32, (devices, LANES), 0).astype(F32)
    carry = jnp.zeros((devices, 1), F32)
    for b in range(count // LANES):
        hit = target_row[:, b * LANES : (b + 1) * LANES] == peers
        tally = jnp.dot(hit.astype(F32).astype(BF16), upper, preferred_element_type=F32) + carry
        key[:, b * LANES : (b + 1) * LANES] = jnp.where(hit, tally - 1.0, -1.0)
        carry = tally[:, LANES - 1 : LANES]

    slot_ids = lax.broadcasted_iota(jnp.int32, (capacity, count), 0).astype(F32)

    def build(side):
        @pl.loop(side * group, (side + 1) * group)
        def _(p):
            chosen = key[pl.ds(p, 1), :] == slot_ids
            pack[pl.ds(pl.multiple_of(p * capacity, capacity), capacity), :] = jnp.where(
                chosen, 1.0, 0.0
            ).astype(BF16)

    def chunk(i):
        return pl.ds(pl.multiple_of(i * capacity, capacity), capacity)

    def remote(e, peer, crossing):
        return pltpu.make_async_remote_copy(
            src_ref=send.at[e, chunk(peer)],
            dst_ref=recv.at[e, chunk(me)],
            send_sem=send_sem.at[e],
            recv_sem=recv_sem.at[e, crossing],
            device_id={"sub": peer},
            device_id_type=pl.DeviceIdType.MESH,
        )

    def whole(e, crossing, chunks):
        at = pl.ds(0, chunks * capacity)
        return pltpu.make_async_remote_copy(
            src_ref=send.at[e, at],
            dst_ref=recv.at[e, at],
            send_sem=send_sem.at[e],
            recv_sem=recv_sem.at[e, crossing],
            device_id={"sub": flipped(me, 1, devices)},
            device_id_type=pl.DeviceIdType.MESH,
        )

    def exchange(e, h, new=False):
        @pl.loop(0, parts)
        def _(i):
            far = parts - 1 - i
            side = flipped(part, far, parts)
            if new:

                @pl.when(i > 0)
                def _():
                    build(side)

            at = pl.ds(pl.multiple_of(side * piece, piece), piece)
            send[e, at, :] = jnp.dot(pack[at, :], low[h], preferred_element_type=F32).astype(BF16)
            each_peer(far, lambda peer: remote(e, peer, far * 2 // parts).start())

    def wait_near(e):
        whole(e, 0, devices // 2 - 1).wait_recv()

    def wait_far(e):
        whole(e, 1, devices // 2).wait_recv()

    gap_copy.wait()
    for h in range(halves):
        for s in range(subs):
            values = gap[s, :, h * LANES : (h + 1) * LANES]
            low[h, s * rows : (s + 1) * rows, :] = values
    build(flipped(part, parts - 1, parts))
    pl.semaphore_wait(barrier, devices - 1)
    for h in range(halves):
        exchange(h, h, h == 0)

    for h in range(halves):
        for s in range(subs):
            term[h, s * rows : (s + 1) * rows, :] = low[h, s * rows : (s + 1) * rows, :].astype(F32)
    mu[...] = jnp.zeros_like(mu)

    bands = rows // LANES
    tile = dof // bands
    lanes = lax.broadcasted_iota(jnp.int32, (LANES, LANES), 1).astype(F32)
    sublanes = lax.broadcasted_iota(jnp.int32, (LANES, LANES), 0)

    def find(s, j):
        base = s * rows + j * LANES
        at = pl.ds(pl.multiple_of(base, LANES), LANES)
        mine = partners[pl.ds(s, 1), pl.ds(pl.multiple_of(j * LANES, LANES), LANES)].astype(F32)
        across = jnp.transpose(jnp.broadcast_to(mine, (LANES, LANES)))
        target = jnp.floor((across + 0.5) * (1.0 / count))
        first = target * count
        tally = jnp.zeros((LANES, LANES), F32)
        for c in range(count // LANES):
            other = partner_row[:, c * LANES : (c + 1) * LANES]
            tally = tally + jnp.where((other < across) & (other >= first), 1.0, 0.0)
        slot = target * capacity + jnp.sum(tally, axis=1, keepdims=True)
        own = (sublanes + (me * count + base)).astype(F32)
        sign[at, :] = jnp.where(own < across, 1.0, -1.0)
        for c in range(wide // LANES):
            pick[at, c * LANES : (c + 1) * LANES] = jnp.where(
                slot - c * LANES == lanes, 1.0, 0.0
            ).astype(BF16)

    for s in range(subs):
        cou_copy(s).wait()
        fac_copy(s).wait()
        limit = blocks_ref[s] * DBLK
        present = lax.broadcasted_iota(jnp.int32, (dof, rows), 0) < limit
        turned[...] = jnp.transpose(jnp.where(present, cou[s], jnp.zeros((dof, rows), BF16)))

        @pl.loop(0, bands)
        def _(j):
            at = pl.ds(pl.multiple_of(j * tile, tile), tile)
            product = jnp.dot(turned[...], fac[s, :, at], preferred_element_type=F32)
            find(s, j)
            keep = lax.broadcasted_iota(jnp.int32, (rows, tile), 1) + j * tile < limit
            reduced[:, at] = jnp.where(keep, product, 0.0).astype(BF16)

        panel[s] = lax.dot_general(
            reduced[...], reduced[...], (((1,), (1,)), ((), ())), preferred_element_type=F32
        ).astype(BF16)

    @pl.loop(0, ITERS)
    def _(k):
        for h in range(halves):
            e = k * halves + h
            wait_near(e)
            wait_far(e)

            @pl.loop(0, subs)
            def _(s):
                at = pl.ds(pl.multiple_of(s * rows, rows), rows)
                arrived = jnp.dot(pick[at, :], recv[e], preferred_element_type=F32)
                moved = mu[h, at, :] + STEP_SIZE * (term[h, at, :] - arrived)
                mu[h, at, :] = moved
                image = jnp.dot(panel[s], moved.astype(BF16), preferred_element_type=F32)
                left = gap[s, :, h * LANES : (h + 1) * LANES].astype(F32) - image
                term[h, at, :] = left
                low[h, at, :] = left.astype(BF16)

            exchange(e + halves, h)

    for h in range(halves):
        for s in range(subs):
            at = slice(s * rows, (s + 1) * rows)
            mult_out[s, :, h * LANES : (h + 1) * LANES] = mu[h, at, :] * sign[at, :]

    def sq_remote(h, peer):
        return pltpu.make_async_remote_copy(
            src_ref=sq_send.at[h],
            dst_ref=sq_recv.at[h, me],
            send_sem=sqs_sem.at[h],
            recv_sem=sqr_sem.at[h],
            device_id={"sub": peer},
            device_id_type=pl.DeviceIdType.MESH,
        )

    for h in range(halves):
        e = ITERS * halves + h
        half = slots // 2
        split = wide == slots and half % LANES == 0
        if split:
            side = me // (devices // 2)
            wait_near(e)
            last = pl.ds(pl.multiple_of(side * half, LANES), half)
            for s in range(subs):
                at = slice(s * rows, (s + 1) * rows)
                arrived = jnp.dot(pick[at, last], recv[e, last, :], preferred_element_type=F32)
                term[h, at, :] = term[h, at, :] - arrived
            wait_far(e)
            last = pl.ds(pl.multiple_of((1 - side) * half, LANES), half)
        else:
            wait_near(e)
            wait_far(e)
            last = slice(0, wide)
        total = jnp.zeros((1, LANES), F32)
        for s in range(subs):
            at = slice(s * rows, (s + 1) * rows)
            arrived = jnp.dot(pick[at, last], recv[e, last, :], preferred_element_type=F32)
            left = term[h, at, :] - arrived
            term[h, at, :] = left
            total = total + jnp.sum(left * left, axis=0, keepdims=True)
        total = jnp.broadcast_to(total, (8, LANES))
        sq_send[h] = total
        sq_recv[h, me] = total

        @pl.loop(0, parts)
        def _(i):
            each_peer(parts - 1 - i, lambda peer: sq_remote(h, peer).start())

        for s in range(subs):
            at = slice(s * rows, (s + 1) * rows)
            resid_out[s, :, h * LANES : (h + 1) * LANES] = term[h, at, :] * sign[at, :]

    for e in range((ITERS + 1) * halves):
        whole(e, 0, devices - 1).wait_send()

    def sq_whole(h, wait_recv):
        copy = pltpu.make_async_remote_copy(
            src_ref=sq_recv.at[h, pl.ds(0, devices - 1)],
            dst_ref=sq_recv.at[h, pl.ds(0, devices - 1)],
            send_sem=sqs_sem.at[h],
            recv_sem=sqr_sem.at[h],
            device_id={"sub": flipped(me, 1, devices)},
            device_id_type=pl.DeviceIdType.MESH,
        )
        return copy.wait_recv() if wait_recv else copy.wait_send()

    for h in range(halves):
        sq_whole(h, False)
    for h in range(halves):
        sq_whole(h, True)
        everyone = jnp.sum(sq_recv[h], axis=0)
        rms_out[:, h * LANES : (h + 1) * LANES] = jnp.sqrt(everyone[0:1] / (count * devices) + 1e-06)


def store(mult, resid, rms, mult_out, resid_out, rms_out, sems):
    subs = mult.shape[0]
    copies = [pltpu.make_async_copy(rms, rms_out, sems.at[2 * subs])]
    for s in range(subs):
        copies.append(pltpu.make_async_copy(mult.at[s], mult_out.at[s], sems.at[2 * s]))
        copies.append(pltpu.make_async_copy(resid.at[s], resid_out.at[s], sems.at[2 * s + 1]))
    for copy in copies:
        copy.start()
    for copy in copies:
        copy.wait()


def local(factors, coupling, gap_loads, dof_blocks, partner_rows):
    subs, rows, cases = gap_loads.shape
    dof = factors.shape[1]
    devices = lax.axis_size("sub")
    count = subs * rows
    halves = cases // LANES
    spread = max(devices // 2 - 1, 1)
    capacity = FROWS * ((count // FROWS // 2 + spread - 1) // spread)
    slots = devices * capacity
    wide = -(-slots // LANES) * LANES
    trips = (ITERS + 1) * halves
    vmem = pl.BlockSpec(memory_space=pltpu.VMEM)
    anywhere = pl.BlockSpec(memory_space=pltpu.HBM)
    mult, resid, rms = pl.pallas_call(
        functools.partial(kernel, devices, capacity),
        out_shape=(
            pltpu.VMEM((subs, rows, cases), F32),
            pltpu.VMEM((subs, rows, cases), F32),
            pltpu.VMEM((1, cases), F32),
        ),
        in_specs=[pl.BlockSpec(memory_space=pltpu.SMEM), anywhere, anywhere, anywhere, vmem],
        out_specs=(vmem, vmem, vmem),
        scratch_shapes=[
            pltpu.VMEM((subs, rows, cases), BF16),
            pltpu.VMEM((subs, dof, dof), BF16),
            pltpu.VMEM((subs, dof, rows), BF16),
            pltpu.VMEM((slots, count), BF16),
            pltpu.VMEM((count, wide), BF16),
            pltpu.VMEM((subs, rows, rows), BF16),
            pltpu.VMEM((rows, dof), BF16),
            pltpu.VMEM((rows, dof), BF16),
            pltpu.VMEM((trips, slots, LANES), BF16),
            pltpu.VMEM((trips, wide, LANES), BF16),
            pltpu.VMEM((halves, count, LANES), BF16),
            pltpu.VMEM((halves, count, LANES), F32),
            pltpu.VMEM((halves, count, LANES), F32),
            pltpu.VMEM((count, LANES), F32),
            pltpu.VMEM((devices, count), F32),
            pltpu.VMEM((halves, 8, LANES), F32),
            pltpu.VMEM((halves, devices, 8, LANES), F32),
            pltpu.SemaphoreType.DMA,
            pltpu.SemaphoreType.DMA((subs,)),
            pltpu.SemaphoreType.DMA((subs,)),
            pltpu.SemaphoreType.DMA((trips,)),
            pltpu.SemaphoreType.DMA((trips, 2)),
            pltpu.SemaphoreType.DMA((halves,)),
            pltpu.SemaphoreType.DMA((halves,)),
        ],
        compiler_params=pltpu.CompilerParams(
            collective_id=0, has_side_effects=True, vmem_limit_bytes=58 * 1024 * 1024
        ),
    )(dof_blocks, factors, coupling, gap_loads, partner_rows)
    mult, resid, rms = (pltpu.with_memory_space_constraint(x, pltpu.VMEM) for x in (mult, resid, rms))
    mult, resid, rms = pl.pallas_call(
        store,
        out_shape=(
            jax.ShapeDtypeStruct((subs, rows, cases), F32),
            jax.ShapeDtypeStruct((subs, rows, cases), F32),
            jax.ShapeDtypeStruct((1, cases), F32),
        ),
        in_specs=[vmem, vmem, vmem],
        out_specs=(anywhere, anywhere, anywhere),
        scratch_shapes=[pltpu.SemaphoreType.DMA((2 * subs + 1,))],
        compiler_params=pltpu.CompilerParams(vmem_limit_bytes=1024 * 1024),
    )(mult, resid, rms)
    return mult, resid, rms.reshape(cases)


def solution(mesh):
    return jax.shard_map(
        local,
        mesh=mesh,
        in_specs=(
            P(("grp", "sub"), None, None),
            P(("grp", "sub"), None, None),
            P(("grp", "sub"), None, None),
            P(("grp", "sub")),
            P(("grp", "sub"), None),
        ),
        out_specs=(P(("grp", "sub"), None, None), P(("grp", "sub"), None, None), P("grp")),
        check_vma=False,
    )
```

```python
import functools

import jax
import jax.numpy as jnp
from jax import lax
from jax.experimental import pallas as pl
from jax.experimental.pallas import tpu as pltpu
from jax.sharding import PartitionSpec as P

DBLK = 128
FROWS = 16
ITERS = 3
STEP_SIZE = 0.25
LANES = 128
F32 = jnp.float32
BF16 = jnp.bfloat16


def flipped(me, distance, devices):
    peer = 0
    bit = 1
    while bit < devices:
        peer = peer + bit * ((me // bit + distance // bit) % 2)
        bit *= 2
    return peer


def kernel(
    devices, capacity, blocks_ref, factors, coupling, gap_loads, partners,
    mult_out, resid_out, rms_out,
    gap, fac, cou, pack, pack_low, pick, pick_low, panel, turned, reduced, send, recv, low, term, mu, sign,
    key, sq_send, sq_recv,
    gap_sem, fac_sem, cou_sem, send_sem, recv_sem, sqs_sem, sqr_sem, near_sem, far_sem,
):
    subs, rows, cases = gap.shape
    dof = factors.shape[1]
    count = subs * rows
    halves = cases // LANES
    slots = devices * capacity
    wide = pick.shape[1]
    fold = count // 2
    band = rows // 2
    me = lax.axis_index("sub")
    parts = min(4, devices)
    group = devices // parts
    piece = slots // parts
    part = me // group
    inner = [flipped(me % group, d, group) for d in range(group)]

    middle = (part + 1) // 2 % 2
    outward = part + 1 - 2 * (part % 2)
    inward = parts - 1 - part

    def each_peer(far, action):
        side = flipped(part, far, parts)
        for d in range(group):
            peer = side * group + inner[d]
            if d > 0:
                action(peer)
            else:
                pl.when(far > 0)(functools.partial(action, peer))

    def fac_copy(s):
        return pltpu.make_async_copy(factors.at[s], fac.at[s], fac_sem.at[s])

    def cou_copy(s):
        return pltpu.make_async_copy(coupling.at[s], cou.at[s], cou_sem.at[s])

    gap_copy = pltpu.make_async_copy(gap_loads, gap, gap_sem)
    gap_copy.start()
    cou_copy(0).start()
    fac_copy(0).start()

    barrier = pltpu.get_barrier_semaphore()

    def greet(semaphore, peer):
        pl.semaphore_signal(
            semaphore, inc=1, device_id={"sub": peer}, device_id_type=pl.DeviceIdType.MESH
        )

    def greet_part(side):
        for d in range(group):
            greet(barrier, side * group + inner[d])

    pl.when(middle == 1)(lambda: greet_part(inward))
    greet_part(outward)
    for d in range(1, group):
        greet(barrier, part * group + inner[d])

    def place(i):
        at = pl.multiple_of(i % (devices // 2) * capacity, capacity)
        return i // (devices // 2), pl.ds(at, capacity)

    @pl.loop(0, recv.shape[0])
    def _(e):
        side, at = place(me)
        recv[e, side, at, :] = jnp.zeros((capacity, LANES), BF16)
        if 2 * wide > slots:
            for i in range(2):
                recv[e, i, slots // 2 :, :] = jnp.zeros((wide - slots // 2, LANES), BF16)

    partner_row = jnp.concatenate([partners[s : s + 1, :] for s in range(subs)], axis=1).astype(F32)
    target_row = jnp.floor((partner_row + 0.5) * (1.0 / count))
    upper = (
        lax.broadcasted_iota(jnp.int32, (LANES, LANES), 0)
        <= lax.broadcasted_iota(jnp.int32, (LANES, LANES), 1)
    ).astype(F32).astype(BF16)
    peers = lax.broadcasted_iota(jnp.int32, (devices, LANES), 0).astype(F32)
    carry = jnp.zeros((devices, 1), F32)
    for b in range(count // LANES):
        hit = target_row[:, b * LANES : (b + 1) * LANES] == peers
        tally = jnp.dot(hit.astype(F32).astype(BF16), upper, preferred_element_type=F32) + carry
        key[:, b * LANES : (b + 1) * LANES] = jnp.where(hit, tally - 1.0, -1.0)
        carry = tally[:, LANES - 1 : LANES]

    slot_ids = lax.broadcasted_iota(jnp.int32, (capacity, count), 0).astype(F32)

    def build(side):
        @pl.loop(side * group, (side + 1) * group)
        def _(p):
            chosen = jnp.where(key[pl.ds(p, 1), :] == slot_ids, 1.0, 0.0)
            at = pl.ds(pl.multiple_of(p * capacity, capacity), capacity)
            lower = chosen[:, :fold]
            pack[at, :] = (lower + chosen[:, fold:]).astype(BF16)
            pack_low[at, :] = jnp.broadcast_to(jnp.sum(lower, axis=1, keepdims=True), (capacity, LANES))

    def chunk(i):
        return pl.ds(pl.multiple_of(i * capacity, capacity), capacity)

    def remote(e, peer, crossing):
        return pltpu.make_async_remote_copy(
            src_ref=send.at[e, chunk(peer)],
            dst_ref=recv.at[e, *place(me)],
            send_sem=send_sem.at[e],
            recv_sem=recv_sem.at[e, crossing],
            device_id={"sub": peer},
            device_id_type=pl.DeviceIdType.MESH,
        )

    def arrival(e, crossing, chunks):
        at = pl.ds(0, chunks * capacity)
        return pltpu.make_async_remote_copy(
            src_ref=recv.at[e, crossing, at],
            dst_ref=recv.at[e, crossing, at],
            send_sem=send_sem.at[e],
            recv_sem=recv_sem.at[e, crossing],
            device_id={"sub": flipped(me, 1, devices)},
            device_id_type=pl.DeviceIdType.MESH,
        )

    def departure(e):
        at = pl.ds(0, (devices - 1) * capacity)
        return pltpu.make_async_remote_copy(
            src_ref=send.at[e, at],
            dst_ref=send.at[e, at],
            send_sem=send_sem.at[e],
            recv_sem=recv_sem.at[e, 0],
            device_id={"sub": flipped(me, 1, devices)},
            device_id_type=pl.DeviceIdType.MESH,
        )

    def either(lower, pair):
        return jnp.where(lower > 0.5, pair[:, :LANES], pair[:, LANES:])

    def fill(e, h, side):
        at = pl.ds(pl.multiple_of(side * piece, piece), piece)
        pair = jnp.dot(pack[at, :], low[h], preferred_element_type=F32)
        send[e, at, :] = either(pack_low[at, :], pair).astype(BF16)

    def post(e, far):
        each_peer(far, lambda peer: remote(e, peer, far * 2 // parts).start())

    def wait_all(e):
        arrival(e, 0, devices // 2 - 1).wait_recv()
        arrival(e, 1, devices // 2).wait_recv()

    def lane(h):
        return pl.ds(pl.multiple_of(h * LANES, LANES), LANES)

    def span(s):
        return pl.ds(pl.multiple_of(s * rows, rows), rows)

    def each_sub(body):
        for s in range(subs):
            body(s)

    def each_part(body):
        for i in range(parts):
            body(i)

    def set_low(h, s, values):
        for i in range(2):
            q = 2 * s + i
            at = pl.ds(pl.multiple_of(q % subs * band, band), band)
            low[h, at, lane(q // subs)] = values[i * band : (i + 1) * band, :]

    def get_arrived(e, s):
        both = jnp.concatenate([recv[e, 0], recv[e, 1]], axis=1)
        pair = jnp.dot(pick[span(s), :], both, preferred_element_type=F32)
        return either(pick_low[span(s), :], pair)

    gap_copy.wait()
    for h in range(halves):
        for s in range(subs):
            values = gap[s, :, h * LANES : (h + 1) * LANES]
            set_low(h, s, values)
    def turn(i):
        return middle * (parts - 1 - i) + (1 - middle) * ((i + 1) % parts)

    build(flipped(part, turn(0), parts))
    pl.semaphore_wait(barrier, (2 + middle) * group - 1)

    @pl.when(middle == 1)
    def _():
        greet(near_sem, inward * group + inner[0])
        greet(near_sem, outward * group + inner[0])

    def begin(h, i):
        fill(h, h, flipped(part, turn(i), parts))
        post(h, turn(i))

    @pl.loop(0, parts * halves)
    def _(t):
        first = t // halves == 0
        u = jnp.maximum(t - halves, 0)
        h = jnp.where(first, t, u // (parts - 1))
        i = jnp.where(first, 0, u % (parts - 1) + 1)

        @pl.when((t >= halves) & (h == 0))
        def _():
            build(flipped(part, turn(i), parts))

        @pl.when(t == halves)
        def _():
            pl.semaphore_wait(near_sem, 1)
            pl.when(middle == 1)(lambda: greet(far_sem, outward * group + inner[0]))

        @pl.when((t == halves + 1) & (middle == 0))
        def _():
            pl.semaphore_wait(far_sem, 1)

        begin(h, i)

    for h in range(halves):
        for s in range(subs):
            term[h, s * rows : (s + 1) * rows, :] = gap[s, :, h * LANES : (h + 1) * LANES].astype(F32)
    mu[...] = jnp.zeros_like(mu)

    bands = rows // LANES
    tile = dof // bands
    lanes = lax.broadcasted_iota(jnp.int32, (LANES, LANES), 1).astype(F32)
    sublanes = lax.broadcasted_iota(jnp.int32, (LANES, LANES), 0)

    def find(s, j):
        base = s * rows + j * LANES
        at = pl.ds(pl.multiple_of(base, LANES), LANES)
        mine = partners[pl.ds(s, 1), pl.ds(pl.multiple_of(j * LANES, LANES), LANES)].astype(F32)
        across = jnp.transpose(jnp.broadcast_to(mine, (LANES, LANES)))
        target = jnp.floor((across + 0.5) * (1.0 / count))
        first = target * count
        tally = jnp.zeros((LANES, LANES), F32)
        for c in range(count // LANES):
            other = partner_row[:, c * LANES : (c + 1) * LANES]
            tally = tally + jnp.where((other < across) & (other >= first), 1.0, 0.0)
        slot = target * capacity + jnp.sum(tally, axis=1, keepdims=True)
        own = (sublanes + (me * count + base)).astype(F32)
        sign[at, :] = jnp.where(own < across, 1.0, -1.0)
        half = slots // 2
        lower = slot < half
        slot = jnp.where(lower, slot, slot - half)
        pick_low[at, :] = jnp.broadcast_to(jnp.where(lower, 1.0, 0.0), (LANES, LANES))
        for c in range(wide // LANES):
            pick[at, c * LANES : (c + 1) * LANES] = jnp.where(
                slot - c * LANES == lanes, 1.0, 0.0
            ).astype(BF16)

    for s in range(subs):
        cou_copy(s).wait()
        fac_copy(s).wait()
        if s + 1 < subs:
            cou_copy(s + 1).start()
            fac_copy(s + 1).start()
        limit = blocks_ref[s] * DBLK
        present = lax.broadcasted_iota(jnp.int32, (dof, rows), 0) < limit
        turned[...] = jnp.transpose(jnp.where(present, cou[s], jnp.zeros((dof, rows), BF16)))

        @pl.loop(0, bands)
        def _(j):
            at = pl.ds(pl.multiple_of(j * tile, tile), tile)
            product = jnp.dot(turned[...], fac[s, :, at], preferred_element_type=F32)
            find(s, j)
            keep = lax.broadcasted_iota(jnp.int32, (rows, tile), 1) + j * tile < limit
            reduced[:, at] = jnp.where(keep, product, 0.0).astype(BF16)

        panel[s] = lax.dot_general(
            reduced[...], reduced[...], (((1,), (1,)), ((), ())), preferred_element_type=F32
        ).astype(BF16)

    @pl.loop(0, ITERS * halves)
    def _(e):
        h = e % halves
        wait_all(e)

        @each_sub
        def _(s):
            at = span(s)
            arrived = get_arrived(e, s)
            moved = mu[h, at, :] + STEP_SIZE * (term[h, at, :] - arrived)
            mu[h, at, :] = moved
            image = jnp.dot(panel[s], moved.astype(BF16), preferred_element_type=F32)
            left = gap[s, :, lane(h)].astype(F32) - image
            term[h, at, :] = left
            set_low(h, s, left.astype(BF16))

        @each_part
        def _(i):
            far = parts - 1 - i
            fill(e + halves, h, flipped(part, far, parts))
            post(e + halves, far)

    @pl.loop(0, halves)
    def _(h):
        @pl.loop(0, subs)
        def _(s):
            mult_out[s, :, lane(h)] = mu[h, span(s), :] * sign[span(s), :]

    def sq_remote(h, peer):
        return pltpu.make_async_remote_copy(
            src_ref=sq_send.at[h],
            dst_ref=sq_recv.at[h, me],
            send_sem=sqs_sem.at[h],
            recv_sem=sqr_sem.at[h],
            device_id={"sub": peer},
            device_id_type=pl.DeviceIdType.MESH,
        )

    @pl.loop(0, halves)
    def _(h):
        e = ITERS * halves + h
        sq_send[h] = jnp.zeros((8, LANES), F32)
        wait_all(e)

        @each_sub
        def _(s):
            left = term[h, span(s), :] - get_arrived(e, s)
            term[h, span(s), :] = left
            sq_send[h] = sq_send[h] + jnp.sum((left * left).reshape(rows // 8, 8, LANES), axis=0)

        sq_recv[h, me] = sq_send[h]

        @pl.loop(0, parts)
        def _(i):
            each_peer(parts - 1 - i, lambda peer: sq_remote(h, peer).start())

        @pl.loop(0, subs)
        def _(s):
            resid_out[s, :, lane(h)] = term[h, span(s), :] * sign[span(s), :]

    @pl.loop(0, (ITERS + 1) * halves)
    def _(e):
        departure(e).wait_send()

    def sq_whole(h, wait_recv):
        copy = pltpu.make_async_remote_copy(
            src_ref=sq_recv.at[h, pl.ds(0, devices - 1)],
            dst_ref=sq_recv.at[h, pl.ds(0, devices - 1)],
            send_sem=sqs_sem.at[h],
            recv_sem=sqr_sem.at[h],
            device_id={"sub": flipped(me, 1, devices)},
            device_id_type=pl.DeviceIdType.MESH,
        )
        return copy.wait_recv() if wait_recv else copy.wait_send()

    for h in range(halves):
        sq_whole(h, False)
    for h in range(halves):
        sq_whole(h, True)
        everyone = jnp.sum(sq_recv[h], axis=0)
        everyone = jnp.sum(everyone, axis=0, keepdims=True)
        rms_out[:, h * LANES : (h + 1) * LANES] = jnp.sqrt(everyone / (count * devices) + 1e-06)


def store(mult, resid, rms, mult_out, resid_out, rms_out, sems):
    subs = mult.shape[0]
    copies = [pltpu.make_async_copy(rms, rms_out, sems.at[2 * subs])]
    for s in range(subs):
        copies.append(pltpu.make_async_copy(mult.at[s], mult_out.at[s], sems.at[2 * s]))
        copies.append(pltpu.make_async_copy(resid.at[s], resid_out.at[s], sems.at[2 * s + 1]))
    for copy in copies:
        copy.start()
    for copy in copies:
        copy.wait()


def local(factors, coupling, gap_loads, dof_blocks, partner_rows):
    subs, rows, cases = gap_loads.shape
    dof = factors.shape[1]
    devices = lax.axis_size("sub")
    count = subs * rows
    halves = cases // LANES
    spread = max(devices // 2 - 1, 1)
    capacity = FROWS * ((count // FROWS // 2 + spread - 1) // spread)
    slots = devices * capacity
    wide = -(-(slots // 2) // LANES) * LANES
    trips = (ITERS + 1) * halves
    vmem = pl.BlockSpec(memory_space=pltpu.VMEM)
    anywhere = pl.BlockSpec(memory_space=pltpu.HBM)
    mult, resid, rms = pl.pallas_call(
        functools.partial(kernel, devices, capacity),
        out_shape=(
            pltpu.VMEM((subs, rows, cases), F32),
            pltpu.VMEM((subs, rows, cases), F32),
            pltpu.VMEM((1, cases), F32),
        ),
        in_specs=[pl.BlockSpec(memory_space=pltpu.SMEM), anywhere, anywhere, anywhere, vmem],
        out_specs=(vmem, vmem, vmem),
        scratch_shapes=[
            pltpu.VMEM((subs, rows, cases), BF16),
            pltpu.VMEM((subs, dof, dof), BF16),
            pltpu.VMEM((subs, dof, rows), BF16),
            pltpu.VMEM((slots, count // 2), BF16),
            pltpu.VMEM((slots, LANES), F32),
            pltpu.VMEM((count, wide), BF16),
            pltpu.VMEM((count, LANES), F32),
            pltpu.VMEM((subs, rows, rows), BF16),
            pltpu.VMEM((rows, dof), BF16),
            pltpu.VMEM((rows, dof), BF16),
            pltpu.VMEM((trips, slots, LANES), BF16),
            pltpu.VMEM((trips, 2, wide, LANES), BF16),
            pltpu.VMEM((halves, count // 2, 2 * LANES), BF16),
            pltpu.VMEM((halves, count, LANES), F32),
            pltpu.VMEM((halves, count, LANES), F32),
            pltpu.VMEM((count, LANES), F32),
            pltpu.VMEM((devices, count), F32),
            pltpu.VMEM((halves, 8, LANES), F32),
            pltpu.VMEM((halves, devices, 8, LANES), F32),
            pltpu.SemaphoreType.DMA,
            pltpu.SemaphoreType.DMA((subs,)),
            pltpu.SemaphoreType.DMA((subs,)),
            pltpu.SemaphoreType.DMA((trips,)),
            pltpu.SemaphoreType.DMA((trips, 2)),
            pltpu.SemaphoreType.DMA((halves,)),
            pltpu.SemaphoreType.DMA((halves,)),
            pltpu.SemaphoreType.REGULAR,
            pltpu.SemaphoreType.REGULAR,
        ],
        compiler_params=pltpu.CompilerParams(
            collective_id=0, has_side_effects=True, vmem_limit_bytes=58 * 1024 * 1024
        ),
    )(dof_blocks, factors, coupling, gap_loads, partner_rows)
    mult, resid, rms = (pltpu.with_memory_space_constraint(x, pltpu.VMEM) for x in (mult, resid, rms))
    mult, resid, rms = pl.pallas_call(
        store,
        out_shape=(
            jax.ShapeDtypeStruct((subs, rows, cases), F32),
            jax.ShapeDtypeStruct((subs, rows, cases), F32),
            jax.ShapeDtypeStruct((1, cases), F32),
        ),
        in_specs=[vmem, vmem, vmem],
        out_specs=(anywhere, anywhere, anywhere),
        scratch_shapes=[pltpu.SemaphoreType.DMA((2 * subs + 1,))],
        compiler_params=pltpu.CompilerParams(vmem_limit_bytes=1024 * 1024),
    )(mult, resid, rms)
    return mult, resid, rms.reshape(cases)


def solution(mesh):
    return jax.shard_map(
        local,
        mesh=mesh,
        in_specs=(
            P(("grp", "sub"), None, None),
            P(("grp", "sub"), None, None),
            P(("grp", "sub"), None, None),
            P(("grp", "sub")),
            P(("grp", "sub"), None),
        ),
        out_specs=(P(("grp", "sub"), None, None), P(("grp", "sub"), None, None), P("grp")),
        check_vma=False,
    )
```

```python
import functools

import jax
import jax.numpy as jnp
from jax import lax
from jax.experimental import pallas as pl
from jax.experimental.pallas import tpu as pltpu
from jax.sharding import PartitionSpec as P

DBLK = 128
FROWS = 16
ITERS = 3
STEP_SIZE = 0.25
LANES = 128
F32 = jnp.float32
BF16 = jnp.bfloat16


def flipped(me, distance, devices):
    peer = 0
    bit = 1
    while bit < devices:
        peer = peer + bit * ((me // bit + distance // bit) % 2)
        bit *= 2
    return peer


def kernel(
    devices, capacity, blocks_ref, factors, coupling, gap_loads, partners,
    mult_out, resid_out, rms_out,
    gap, fac, cou, pack, pack_low, pick, pick_low, panel, turned, reduced, send, recv, low, term, mu, sign, weight, early,
    key, sq_send, sq_recv,
    gap_sem, fac_sem, cou_sem, send_sem, recv_sem, sqs_sem, sqr_sem, near_sem, far_sem,
):
    subs, rows, cases = gap.shape
    dof = factors.shape[1]
    count = subs * rows
    halves = cases // LANES
    slots = devices * capacity
    wide = pick.shape[1]
    fold = count // 2
    band = rows // 2
    me = lax.axis_index("sub")
    parts = min(4, devices)
    group = devices // parts
    piece = slots // parts
    part = me // group
    inner = [flipped(me % group, d, group) for d in range(group)]

    middle = (part + 1) // 2 % 2
    outward = part + 1 - 2 * (part % 2)
    inward = parts - 1 - part
    upper_half = part // 2
    first_far = 3 - upper_half
    second_far = 2 + upper_half
    first_source = flipped(part, second_far, parts)

    def each_peer(far, action):
        side = flipped(part, far, parts)
        for d in range(group):
            peer = side * group + inner[d]
            if d > 0:
                action(peer)
            else:
                pl.when(far > 0)(functools.partial(action, peer))

    def fac_copy(s):
        return pltpu.make_async_copy(factors.at[s], fac.at[s], fac_sem.at[s])

    def cou_copy(s):
        return pltpu.make_async_copy(coupling.at[s], cou.at[s], cou_sem.at[s])

    gap_copy = pltpu.make_async_copy(gap_loads, gap, gap_sem)
    gap_copy.start()
    cou_copy(0).start()
    fac_copy(0).start()

    barrier = pltpu.get_barrier_semaphore()

    def greet(semaphore, peer):
        pl.semaphore_signal(
            semaphore, inc=1, device_id={"sub": peer}, device_id_type=pl.DeviceIdType.MESH
        )

    def greet_part(side):
        for d in range(group):
            greet(barrier, side * group + inner[d])

    pl.when(middle == 1)(lambda: greet_part(inward))
    greet_part(outward)
    for d in range(1, group):
        greet(barrier, part * group + inner[d])

    def place(i):
        at = pl.multiple_of(i % (devices // 2) * capacity, capacity)
        return i // (devices // 2), pl.ds(at, capacity)

    @pl.loop(0, recv.shape[0])
    def _(e):
        side, at = place(me)
        recv[e, side, at, :] = jnp.zeros((capacity, LANES), BF16)
        if 2 * wide > slots:
            for i in range(2):
                recv[e, i, slots // 2 :, :] = jnp.zeros((wide - slots // 2, LANES), BF16)

    partner_row = jnp.concatenate([partners[s : s + 1, :] for s in range(subs)], axis=1).astype(F32)
    target_row = jnp.floor((partner_row + 0.5) * (1.0 / count))
    upper = (
        lax.broadcasted_iota(jnp.int32, (LANES, LANES), 0)
        <= lax.broadcasted_iota(jnp.int32, (LANES, LANES), 1)
    ).astype(F32).astype(BF16)
    peers = lax.broadcasted_iota(jnp.int32, (devices, LANES), 0).astype(F32)
    carry = jnp.zeros((devices, 1), F32)
    for b in range(count // LANES):
        hit = target_row[:, b * LANES : (b + 1) * LANES] == peers
        tally = jnp.dot(hit.astype(F32).astype(BF16), upper, preferred_element_type=F32) + carry
        key[:, b * LANES : (b + 1) * LANES] = jnp.where(hit, tally - 1.0, -1.0)
        carry = tally[:, LANES - 1 : LANES]

    slot_ids = lax.broadcasted_iota(jnp.int32, (capacity, count), 0).astype(F32)

    def build(side):
        @pl.loop(side * group, (side + 1) * group)
        def _(p):
            chosen = jnp.where(key[pl.ds(p, 1), :] == slot_ids, 1.0, 0.0)
            at = pl.ds(pl.multiple_of(p * capacity, capacity), capacity)
            lower = chosen[:, :fold]
            pack[at, :] = (lower + chosen[:, fold:]).astype(BF16)
            pack_low[at, :] = jnp.broadcast_to(jnp.sum(lower, axis=1, keepdims=True), (capacity, LANES))

    def chunk(i):
        return pl.ds(pl.multiple_of(i * capacity, capacity), capacity)

    def remote(e, peer, crossing):
        return pltpu.make_async_remote_copy(
            src_ref=send.at[e, chunk(peer)],
            dst_ref=recv.at[e, *place(me)],
            send_sem=send_sem.at[e],
            recv_sem=recv_sem.at[e, crossing],
            device_id={"sub": peer},
            device_id_type=pl.DeviceIdType.MESH,
        )

    def arrival(e, crossing, chunks):
        at = pl.ds(0, chunks * capacity)
        return pltpu.make_async_remote_copy(
            src_ref=recv.at[e, 0, at],
            dst_ref=recv.at[e, 0, at],
            send_sem=send_sem.at[e],
            recv_sem=recv_sem.at[e, crossing],
            device_id={"sub": flipped(me, 1, devices)},
            device_id_type=pl.DeviceIdType.MESH,
        )

    def departure(e):
        at = pl.ds(0, (devices - 1) * capacity)
        return pltpu.make_async_remote_copy(
            src_ref=send.at[e, at],
            dst_ref=send.at[e, at],
            send_sem=send_sem.at[e],
            recv_sem=recv_sem.at[e, 0],
            device_id={"sub": flipped(me, 1, devices)},
            device_id_type=pl.DeviceIdType.MESH,
        )

    def either(lower, pair):
        return jnp.where(lower > 0.5, pair[:, :LANES], pair[:, LANES:])

    def fill(e, h, side):
        at = pl.ds(pl.multiple_of(side * piece, piece), piece)
        pair = jnp.dot(pack[at, :], low[h], preferred_element_type=F32)
        send[e, at, :] = either(pack_low[at, :], pair).astype(BF16)

    def post(e, far):
        crossing = jnp.where(far < parts // 2, 0, jnp.where(far == first_far, 1, 2))
        each_peer(far, lambda peer: remote(e, peer, crossing).start())

    def wait_first(e):
        arrival(e, 0, devices // 2 - 1).wait_recv()
        arrival(e, 1, group).wait_recv()

    def wait_rest(e):
        arrival(e, 2, group).wait_recv()

    def lane(h):
        return pl.ds(pl.multiple_of(h * LANES, LANES), LANES)

    def span(s):
        return pl.ds(pl.multiple_of(s * rows, rows), rows)

    def quarter(i):
        return pl.ds(pl.multiple_of(i * (slots // 4), capacity), slots // 4)

    def each_sub(body):
        for s in range(subs):
            body(s)

    def each_part(body):
        for i in range(parts):
            body(i)

    def set_low(h, s, values):
        for i in range(2):
            q = 2 * s + i
            at = pl.ds(pl.multiple_of(q % subs * band, band), band)
            low[h, at, lane(q // subs)] = values[i * band : (i + 1) * band, :]

    def get_arrived(source, s):
        both = jnp.concatenate([source[0], source[1]], axis=1)
        pair = jnp.dot(pick[span(s), :], both, preferred_element_type=F32)
        return either(pick_low[span(s), :], pair)

    gap_copy.wait()
    for h in range(halves):
        for s in range(subs):
            values = gap[s, :, h * LANES : (h + 1) * LANES]
            set_low(h, s, values)
    def turn(i):
        return middle * (parts - 1 - i) + (1 - middle) * ((i + 1) % parts)

    build(flipped(part, turn(0), parts))
    pl.semaphore_wait(barrier, (2 + middle) * group - 1)

    @pl.when(middle == 1)
    def _():
        greet(near_sem, inward * group + inner[0])
        greet(near_sem, outward * group + inner[0])

    def begin(h, i):
        fill(h, h, flipped(part, turn(i), parts))
        post(h, turn(i))

    @pl.loop(0, parts * halves)
    def _(t):
        first = t // halves == 0
        u = jnp.maximum(t - halves, 0)
        h = jnp.where(first, t, u // (parts - 1))
        i = jnp.where(first, 0, u % (parts - 1) + 1)

        @pl.when((t >= halves) & (h == 0))
        def _():
            build(flipped(part, turn(i), parts))

        @pl.when(t == halves)
        def _():
            pl.semaphore_wait(near_sem, 1)
            pl.when(middle == 1)(lambda: greet(far_sem, outward * group + inner[0]))

        @pl.when((t == halves + 1) & (middle == 0))
        def _():
            pl.semaphore_wait(far_sem, 1)

        begin(h, i)

    for h in range(halves):
        for s in range(subs):
            term[h, s * rows : (s + 1) * rows, :] = gap[s, :, h * LANES : (h + 1) * LANES].astype(F32)
    mu[...] = jnp.zeros_like(mu)

    bands = rows // LANES
    tile = dof // bands
    lanes = lax.broadcasted_iota(jnp.int32, (LANES, LANES), 1).astype(F32)
    sublanes = lax.broadcasted_iota(jnp.int32, (LANES, LANES), 0)

    def find(s, j):
        base = s * rows + j * LANES
        at = pl.ds(pl.multiple_of(base, LANES), LANES)
        mine = partners[pl.ds(s, 1), pl.ds(pl.multiple_of(j * LANES, LANES), LANES)].astype(F32)
        across = jnp.transpose(jnp.broadcast_to(mine, (LANES, LANES)))
        target = jnp.floor((across + 0.5) * (1.0 / count))
        first = target * count
        tally = jnp.zeros((LANES, LANES), F32)
        for c in range(count // LANES):
            other = partner_row[:, c * LANES : (c + 1) * LANES]
            tally = tally + jnp.where((other < across) & (other >= first), 1.0, 0.0)
        slot = target * capacity + jnp.sum(tally, axis=1, keepdims=True)
        own = (sublanes + (me * count + base)).astype(F32)
        sign[at, :] = jnp.where(own < across, 1.0, -1.0)
        low_near = (upper_half * (devices // 2)).astype(F32)
        near = (target >= low_near) & (target < low_near + devices // 2)
        low_first = (first_source * group).astype(F32)
        soon = (target >= low_first) & (target < low_first + group)
        weight[at, :] = jnp.where(near, 1.0, jnp.where(soon, 2.0, 0.0))
        half = slots // 2
        lower = slot < half
        slot = jnp.where(lower, slot, slot - half)
        pick_low[at, :] = jnp.broadcast_to(jnp.where(lower, 1.0, 0.0), (LANES, LANES))
        for c in range(wide // LANES):
            pick[at, c * LANES : (c + 1) * LANES] = jnp.where(
                slot - c * LANES == lanes, 1.0, 0.0
            ).astype(BF16)

    for s in range(subs):
        cou_copy(s).wait()
        fac_copy(s).wait()
        if s + 1 < subs:
            cou_copy(s + 1).start()
            fac_copy(s + 1).start()
        limit = blocks_ref[s] * DBLK
        present = lax.broadcasted_iota(jnp.int32, (dof, rows), 0) < limit
        turned[...] = jnp.transpose(jnp.where(present, cou[s], jnp.zeros((dof, rows), BF16)))

        @pl.loop(0, bands)
        def _(j):
            at = pl.ds(pl.multiple_of(j * tile, tile), tile)
            product = jnp.dot(turned[...], fac[s, :, at], preferred_element_type=F32)
            find(s, j)
            keep = lax.broadcasted_iota(jnp.int32, (rows, tile), 1) + j * tile < limit
            reduced[:, at] = jnp.where(keep, product, 0.0).astype(BF16)

        panel[s] = lax.dot_general(
            reduced[...], reduced[...], (((1,), (1,)), ((), ())), preferred_element_type=F32
        ).astype(BF16)

    @pl.loop(0, ITERS * halves)
    def _(e):
        h = e % halves
        wait_first(e)
        wait_rest(e)

        @each_sub
        def _(s):
            at = span(s)
            arrived = get_arrived(recv.at[e], s)
            moved = mu[h, at, :] + STEP_SIZE * (term[h, at, :] - arrived)
            mu[h, at, :] = moved
            image = jnp.dot(panel[s], moved.astype(BF16), preferred_element_type=F32)
            left = gap[s, :, lane(h)].astype(F32) - image
            term[h, at, :] = left
            set_low(h, s, left.astype(BF16))

        @each_part
        def _(i):
            far = jnp.where(e < (ITERS - 1) * halves, parts - 1 - i, (1, 0, first_far, second_far)[i])
            fill(e + halves, h, flipped(part, far, parts))
            post(e + halves, far)

    @pl.loop(0, halves)
    def _(h):
        @pl.loop(0, subs)
        def _(s):
            mult_out[s, :, lane(h)] = mu[h, span(s), :] * sign[span(s), :]

    def sq_remote(h, peer):
        return pltpu.make_async_remote_copy(
            src_ref=sq_send.at[h],
            dst_ref=sq_recv.at[h, me],
            send_sem=sqs_sem.at[h],
            recv_sem=sqr_sem.at[h],
            device_id={"sub": peer},
            device_id_type=pl.DeviceIdType.MESH,
        )

    @pl.loop(0, halves)
    def _(h):
        e = ITERS * halves + h
        sq_send[h] = jnp.zeros((8, LANES), F32)
        wait_first(e)
        early[upper_half] = recv[e, upper_half]
        early[1 - upper_half, quarter(middle), :] = recv[e, 1 - upper_half, quarter(middle), :]
        early[1 - upper_half, quarter(1 - middle), :] = jnp.zeros((slots // 4, LANES), BF16)
        if 2 * wide > slots:
            early[1 - upper_half, slots // 2 :, :] = jnp.zeros((wide - slots // 2, LANES), BF16)

        @each_sub
        def _(s):
            left = term[h, span(s), :] - get_arrived(early, s)
            squares = left * left * weight[span(s), :]
            sq_send[h] = sq_send[h] + jnp.sum(squares.reshape(rows // 8, 8, LANES), axis=0)

        sq_recv[h, me] = sq_send[h]

        @pl.loop(0, parts)
        def _(i):
            each_peer(parts - 1 - i, lambda peer: sq_remote(h, peer).start())

        wait_rest(e)

        @each_sub
        def _(s):
            left = term[h, span(s), :] - get_arrived(recv.at[e], s)
            resid_out[s, :, lane(h)] = left * sign[span(s), :]

    @pl.loop(0, (ITERS + 1) * halves)
    def _(e):
        departure(e).wait_send()

    def sq_whole(h, wait_recv):
        copy = pltpu.make_async_remote_copy(
            src_ref=sq_recv.at[h, pl.ds(0, devices - 1)],
            dst_ref=sq_recv.at[h, pl.ds(0, devices - 1)],
            send_sem=sqs_sem.at[h],
            recv_sem=sqr_sem.at[h],
            device_id={"sub": flipped(me, 1, devices)},
            device_id_type=pl.DeviceIdType.MESH,
        )
        return copy.wait_recv() if wait_recv else copy.wait_send()

    for h in range(halves):
        sq_whole(h, False)
    for h in range(halves):
        sq_whole(h, True)
        everyone = jnp.sum(sq_recv[h], axis=0)
        everyone = jnp.sum(everyone, axis=0, keepdims=True)
        rms_out[:, h * LANES : (h + 1) * LANES] = jnp.sqrt(everyone / (count * devices) + 1e-06)


def store(mult, resid, rms, mult_out, resid_out, rms_out, sems):
    subs = mult.shape[0]
    copies = [pltpu.make_async_copy(rms, rms_out, sems.at[2 * subs])]
    for s in range(subs):
        copies.append(pltpu.make_async_copy(mult.at[s], mult_out.at[s], sems.at[2 * s]))
        copies.append(pltpu.make_async_copy(resid.at[s], resid_out.at[s], sems.at[2 * s + 1]))
    for copy in copies:
        copy.start()
    for copy in copies:
        copy.wait()


def local(factors, coupling, gap_loads, dof_blocks, partner_rows):
    subs, rows, cases = gap_loads.shape
    dof = factors.shape[1]
    devices = lax.axis_size("sub")
    count = subs * rows
    halves = cases // LANES
    spread = max(devices // 2 - 1, 1)
    capacity = FROWS * ((count // FROWS // 2 + spread - 1) // spread)
    slots = devices * capacity
    wide = -(-(slots // 2) // LANES) * LANES
    trips = (ITERS + 1) * halves
    vmem = pl.BlockSpec(memory_space=pltpu.VMEM)
    anywhere = pl.BlockSpec(memory_space=pltpu.HBM)
    mult, resid, rms = pl.pallas_call(
        functools.partial(kernel, devices, capacity),
        out_shape=(
            pltpu.VMEM((subs, rows, cases), F32),
            pltpu.VMEM((subs, rows, cases), F32),
            pltpu.VMEM((1, cases), F32),
        ),
        in_specs=[pl.BlockSpec(memory_space=pltpu.SMEM), anywhere, anywhere, anywhere, vmem],
        out_specs=(vmem, vmem, vmem),
        scratch_shapes=[
            pltpu.VMEM((subs, rows, cases), BF16),
            pltpu.VMEM((subs, dof, dof), BF16),
            pltpu.VMEM((subs, dof, rows), BF16),
            pltpu.VMEM((slots, count // 2), BF16),
            pltpu.VMEM((slots, LANES), F32),
            pltpu.VMEM((count, wide), BF16),
            pltpu.VMEM((count, LANES), F32),
            pltpu.VMEM((subs, rows, rows), BF16),
            pltpu.VMEM((rows, dof), BF16),
            pltpu.VMEM((rows, dof), BF16),
            pltpu.VMEM((trips, slots, LANES), BF16),
            pltpu.VMEM((trips, 2, wide, LANES), BF16),
            pltpu.VMEM((halves, count // 2, 2 * LANES), BF16),
            pltpu.VMEM((halves, count, LANES), F32),
            pltpu.VMEM((halves, count, LANES), F32),
            pltpu.VMEM((count, LANES), F32),
            pltpu.VMEM((count, LANES), F32),
            pltpu.VMEM((2, wide, LANES), BF16),
            pltpu.VMEM((devices, count), F32),
            pltpu.VMEM((halves, 8, LANES), F32),
            pltpu.VMEM((halves, devices, 8, LANES), F32),
            pltpu.SemaphoreType.DMA,
            pltpu.SemaphoreType.DMA((subs,)),
            pltpu.SemaphoreType.DMA((subs,)),
            pltpu.SemaphoreType.DMA((trips,)),
            pltpu.SemaphoreType.DMA((trips, 3)),
            pltpu.SemaphoreType.DMA((halves,)),
            pltpu.SemaphoreType.DMA((halves,)),
            pltpu.SemaphoreType.REGULAR,
            pltpu.SemaphoreType.REGULAR,
        ],
        compiler_params=pltpu.CompilerParams(
            collective_id=0, has_side_effects=True, vmem_limit_bytes=58 * 1024 * 1024
        ),
    )(dof_blocks, factors, coupling, gap_loads, partner_rows)
    mult, resid, rms = (pltpu.with_memory_space_constraint(x, pltpu.VMEM) for x in (mult, resid, rms))
    mult, resid, rms = pl.pallas_call(
        store,
        out_shape=(
            jax.ShapeDtypeStruct((subs, rows, cases), F32),
            jax.ShapeDtypeStruct((subs, rows, cases), F32),
            jax.ShapeDtypeStruct((1, cases), F32),
        ),
        in_specs=[vmem, vmem, vmem],
        out_specs=(anywhere, anywhere, anywhere),
        scratch_shapes=[pltpu.SemaphoreType.DMA((2 * subs + 1,))],
        compiler_params=pltpu.CompilerParams(vmem_limit_bytes=1024 * 1024),
    )(mult, resid, rms)
    return mult, resid, rms.reshape(cases)


def solution(mesh):
    return jax.shard_map(
        local,
        mesh=mesh,
        in_specs=(
            P(("grp", "sub"), None, None),
            P(("grp", "sub"), None, None),
            P(("grp", "sub"), None, None),
            P(("grp", "sub")),
            P(("grp", "sub"), None),
        ),
        out_specs=(P(("grp", "sub"), None, None), P(("grp", "sub"), None, None), P("grp")),
        check_vma=False,
    )
```

```python
import functools

import jax
import jax.numpy as jnp
from jax import lax
from jax.experimental import pallas as pl
from jax.experimental.pallas import tpu as pltpu
from jax.sharding import PartitionSpec as P

DBLK = 128
FROWS = 16
ITERS = 3
STEP_SIZE = 0.25
LANES = 128
F32 = jnp.float32
BF16 = jnp.bfloat16


def flipped(me, distance, devices):
    peer = 0
    bit = 1
    while bit < devices:
        peer = peer + bit * ((me // bit + distance // bit) % 2)
        bit *= 2
    return peer


def kernel(
    devices, capacity, blocks_hbm, factors, coupling, gap_loads, partners_hbm,
    mult_out, resid_out, rms_out,
    gap, fac, cou, pack, pack_low, pick, pick_low, panel, turned, reduced, send, recv, low, term, mu, sign, weight, early,
    key, sq_send, sq_recv,
    gap_sem, fac_sem, cou_sem, send_sem, recv_sem, sqs_sem, sqr_sem, near_sem, far_sem, partners, partners_sem, blocks_ref, blocks_sem,
):
    subs, rows, cases = gap.shape
    dof = factors.shape[1]
    count = subs * rows
    halves = cases // LANES
    slots = devices * capacity
    wide = pick.shape[1]
    fold = count // 2
    band = rows // 2
    me = lax.axis_index("sub")
    parts = min(4, devices)
    group = devices // parts
    piece = slots // parts
    part = me // group
    inner = [flipped(me % group, d, group) for d in range(group)]

    middle = (part + 1) // 2 % 2
    outward = part + 1 - 2 * (part % 2)
    inward = parts - 1 - part
    upper_half = part // 2
    first_far = 3 - upper_half
    second_far = 2 + upper_half
    first_source = flipped(part, second_far, parts)

    def each_peer(far, action):
        side = flipped(part, far, parts)
        for d in range(group):
            peer = side * group + inner[d]
            if d > 0:
                action(peer)
            else:
                pl.when(far > 0)(functools.partial(action, peer))

    def fac_copy(s):
        return pltpu.make_async_copy(factors.at[s], fac.at[s], fac_sem.at[s])

    def cou_copy(s):
        return pltpu.make_async_copy(coupling.at[s], cou.at[s], cou_sem.at[s])

    gap_copy = pltpu.make_async_copy(gap_loads, gap, gap_sem)
    partners_copy = pltpu.make_async_copy(partners_hbm, partners, partners_sem)
    partners_copy.start()
    blocks_copy = pltpu.make_async_copy(blocks_hbm, blocks_ref, blocks_sem)
    blocks_copy.start()
    gap_copy.start()
    cou_copy(0).start()
    fac_copy(0).start()

    barrier = pltpu.get_barrier_semaphore()

    def greet(semaphore, peer):
        pl.semaphore_signal(
            semaphore, inc=1, device_id={"sub": peer}, device_id_type=pl.DeviceIdType.MESH
        )

    def greet_part(side):
        for d in range(group):
            greet(barrier, side * group + inner[d])

    pl.when(middle == 1)(lambda: greet_part(inward))
    greet_part(outward)
    for d in range(1, group):
        greet(barrier, part * group + inner[d])

    def place(i):
        at = pl.multiple_of(i % (devices // 2) * capacity, capacity)
        return i // (devices // 2), pl.ds(at, capacity)

    @pl.loop(0, recv.shape[0])
    def _(e):
        side, at = place(me)
        recv[e, side, at, :] = jnp.zeros((capacity, LANES), BF16)
        if 2 * wide > slots:
            for i in range(2):
                recv[e, i, slots // 2 :, :] = jnp.zeros((wide - slots // 2, LANES), BF16)

    partners_copy.wait()
    partner_row = jnp.concatenate([partners[s : s + 1, :] for s in range(subs)], axis=1).astype(F32)
    target_row = jnp.floor((partner_row + 0.5) * (1.0 / count))
    upper = (
        lax.broadcasted_iota(jnp.int32, (LANES, LANES), 0)
        <= lax.broadcasted_iota(jnp.int32, (LANES, LANES), 1)
    ).astype(F32).astype(BF16)
    peers = lax.broadcasted_iota(jnp.int32, (devices, LANES), 0).astype(F32)
    carry = jnp.zeros((devices, 1), F32)
    for b in range(count // LANES):
        hit = target_row[:, b * LANES : (b + 1) * LANES] == peers
        tally = jnp.dot(hit.astype(F32).astype(BF16), upper, preferred_element_type=F32) + carry
        key[:, b * LANES : (b + 1) * LANES] = jnp.where(hit, tally - 1.0, -1.0)
        carry = tally[:, LANES - 1 : LANES]

    slot_ids = lax.broadcasted_iota(jnp.int32, (capacity, count), 0).astype(F32)

    def build(side):
        @pl.loop(side * group, (side + 1) * group)
        def _(p):
            chosen = jnp.where(key[pl.ds(p, 1), :] == slot_ids, 1.0, 0.0)
            at = pl.ds(pl.multiple_of(p * capacity, capacity), capacity)
            lower = chosen[:, :fold]
            pack[at, :] = (lower + chosen[:, fold:]).astype(BF16)
            pack_low[at, :] = jnp.broadcast_to(jnp.sum(lower, axis=1, keepdims=True), (capacity, LANES))

    def chunk(i):
        return pl.ds(pl.multiple_of(i * capacity, capacity), capacity)

    def remote(e, peer, crossing):
        return pltpu.make_async_remote_copy(
            src_ref=send.at[e, chunk(peer)],
            dst_ref=recv.at[e, *place(me)],
            send_sem=send_sem.at[e],
            recv_sem=recv_sem.at[e, crossing],
            device_id={"sub": peer},
            device_id_type=pl.DeviceIdType.MESH,
        )

    def arrival(e, crossing, chunks):
        at = pl.ds(0, chunks * capacity)
        return pltpu.make_async_remote_copy(
            src_ref=recv.at[e, 0, at],
            dst_ref=recv.at[e, 0, at],
            send_sem=send_sem.at[e],
            recv_sem=recv_sem.at[e, crossing],
            device_id={"sub": flipped(me, 1, devices)},
            device_id_type=pl.DeviceIdType.MESH,
        )

    def departure(e):
        at = pl.ds(0, (devices - 1) * capacity)
        return pltpu.make_async_remote_copy(
            src_ref=send.at[e, at],
            dst_ref=send.at[e, at],
            send_sem=send_sem.at[e],
            recv_sem=recv_sem.at[e, 0],
            device_id={"sub": flipped(me, 1, devices)},
            device_id_type=pl.DeviceIdType.MESH,
        )

    def either(lower, pair):
        return jnp.where(lower > 0.5, pair[:, :LANES], pair[:, LANES:])

    def fill(e, h, side):
        at = pl.ds(pl.multiple_of(side * piece, piece), piece)
        pair = jnp.dot(pack[at, :], low[h], preferred_element_type=F32)
        send[e, at, :] = either(pack_low[at, :], pair).astype(BF16)

    def post(e, far):
        crossing = jnp.where(far < parts // 2, 0, jnp.where(far == first_far, 1, 2))
        each_peer(far, lambda peer: remote(e, peer, crossing).start())

    def wait_first(e):
        arrival(e, 0, devices // 2 - 1).wait_recv()
        arrival(e, 1, group).wait_recv()

    def wait_rest(e):
        arrival(e, 2, group).wait_recv()

    def lane(h):
        return pl.ds(pl.multiple_of(h * LANES, LANES), LANES)

    def span(s):
        return pl.ds(pl.multiple_of(s * rows, rows), rows)

    def quarter(i):
        return pl.ds(pl.multiple_of(i * (slots // 4), capacity), slots // 4)

    def each_sub(body):
        for s in range(subs):
            body(s)

    def each_part(body):
        for i in range(parts):
            body(i)

    def set_low(h, s, values):
        for i in range(2):
            q = 2 * s + i
            at = pl.ds(pl.multiple_of(q % subs * band, band), band)
            low[h, at, lane(q // subs)] = values[i * band : (i + 1) * band, :]

    def get_arrived(source, s):
        both = jnp.concatenate([source[0], source[1]], axis=1)
        pair = jnp.dot(pick[span(s), :], both, preferred_element_type=F32)
        return either(pick_low[span(s), :], pair)

    gap_copy.wait()
    for h in range(halves):
        for s in range(subs):
            values = gap[s, :, h * LANES : (h + 1) * LANES]
            set_low(h, s, values)
    def turn(i):
        return middle * (parts - 1 - i) + (1 - middle) * ((i + 1) % parts)

    build(flipped(part, turn(0), parts))
    pl.semaphore_wait(barrier, (2 + middle) * group - 1)

    @pl.when(middle == 1)
    def _():
        greet(near_sem, inward * group + inner[0])
        greet(near_sem, outward * group + inner[0])

    def begin(h, i):
        fill(h, h, flipped(part, turn(i), parts))
        post(h, turn(i))

    @pl.loop(0, parts * halves)
    def _(t):
        first = t // halves == 0
        u = jnp.maximum(t - halves, 0)
        h = jnp.where(first, t, u // (parts - 1))
        i = jnp.where(first, 0, u % (parts - 1) + 1)

        @pl.when((t >= halves) & (h == 0))
        def _():
            build(flipped(part, turn(i), parts))

        @pl.when(t == halves)
        def _():
            pl.semaphore_wait(near_sem, 1)
            pl.when(middle == 1)(lambda: greet(far_sem, outward * group + inner[0]))

        @pl.when((t == halves + 1) & (middle == 0))
        def _():
            pl.semaphore_wait(far_sem, 1)

        begin(h, i)

    for h in range(halves):
        for s in range(subs):
            term[h, s * rows : (s + 1) * rows, :] = gap[s, :, h * LANES : (h + 1) * LANES].astype(F32)
    mu[...] = jnp.zeros_like(mu)

    bands = rows // LANES
    tile = dof // bands
    lanes = lax.broadcasted_iota(jnp.int32, (LANES, LANES), 1).astype(F32)
    sublanes = lax.broadcasted_iota(jnp.int32, (LANES, LANES), 0)

    def find(s, j):
        base = s * rows + j * LANES
        at = pl.ds(pl.multiple_of(base, LANES), LANES)
        mine = partners[pl.ds(s, 1), pl.ds(pl.multiple_of(j * LANES, LANES), LANES)].astype(F32)
        across = jnp.transpose(jnp.broadcast_to(mine, (LANES, LANES)))
        target = jnp.floor((across + 0.5) * (1.0 / count))
        first = target * count
        tally = jnp.zeros((LANES, LANES), F32)
        for c in range(count // LANES):
            other = partner_row[:, c * LANES : (c + 1) * LANES]
            tally = tally + jnp.where((other < across) & (other >= first), 1.0, 0.0)
        slot = target * capacity + jnp.sum(tally, axis=1, keepdims=True)
        own = (sublanes + (me * count + base)).astype(F32)
        sign[at, :] = jnp.where(own < across, 1.0, -1.0)
        low_near = (upper_half * (devices // 2)).astype(F32)
        near = (target >= low_near) & (target < low_near + devices // 2)
        low_first = (first_source * group).astype(F32)
        soon = (target >= low_first) & (target < low_first + group)
        weight[at, :] = jnp.where(near, 1.0, jnp.where(soon, 2.0, 0.0))
        half = slots // 2
        lower = slot < half
        slot = jnp.where(lower, slot, slot - half)
        pick_low[at, :] = jnp.broadcast_to(jnp.where(lower, 1.0, 0.0), (LANES, LANES))
        for c in range(wide // LANES):
            pick[at, c * LANES : (c + 1) * LANES] = jnp.where(
                slot - c * LANES == lanes, 1.0, 0.0
            ).astype(BF16)

    blocks_copy.wait()
    for s in range(subs):
        cou_copy(s).wait()
        fac_copy(s).wait()
        if s + 1 < subs:
            cou_copy(s + 1).start()
            fac_copy(s + 1).start()
        limit = blocks_ref[s] * DBLK
        present = lax.broadcasted_iota(jnp.int32, (dof, rows), 0) < limit
        turned[...] = jnp.transpose(jnp.where(present, cou[s], jnp.zeros((dof, rows), BF16)))

        @pl.loop(0, bands)
        def _(j):
            at = pl.ds(pl.multiple_of(j * tile, tile), tile)
            product = jnp.dot(turned[...], fac[s, :, at], preferred_element_type=F32)
            find(s, j)
            keep = lax.broadcasted_iota(jnp.int32, (rows, tile), 1) + j * tile < limit
            reduced[:, at] = jnp.where(keep, product, 0.0).astype(BF16)

        panel[s] = lax.dot_general(
            reduced[...], reduced[...], (((1,), (1,)), ((), ())), preferred_element_type=F32
        ).astype(BF16)

    @pl.loop(0, ITERS * halves)
    def _(e):
        h = e % halves
        wait_first(e)
        wait_rest(e)

        @each_sub
        def _(s):
            at = span(s)
            arrived = get_arrived(recv.at[e], s)
            moved = mu[h, at, :] + STEP_SIZE * (term[h, at, :] - arrived)
            mu[h, at, :] = moved
            image = jnp.dot(panel[s], moved.astype(BF16), preferred_element_type=F32)
            left = gap[s, :, lane(h)].astype(F32) - image
            term[h, at, :] = left
            set_low(h, s, left.astype(BF16))

        @each_part
        def _(i):
            far = jnp.where(e < (ITERS - 1) * halves, parts - 1 - i, (1, 0, first_far, second_far)[i])
            fill(e + halves, h, flipped(part, far, parts))
            post(e + halves, far)

    @pl.loop(0, halves)
    def _(h):
        @pl.loop(0, subs)
        def _(s):
            mult_out[s, :, lane(h)] = mu[h, span(s), :] * sign[span(s), :]

    def sq_remote(h, peer):
        return pltpu.make_async_remote_copy(
            src_ref=sq_send.at[h],
            dst_ref=sq_recv.at[h, me],
            send_sem=sqs_sem.at[h],
            recv_sem=sqr_sem.at[h],
            device_id={"sub": peer},
            device_id_type=pl.DeviceIdType.MESH,
        )

    @pl.loop(0, halves)
    def _(h):
        e = ITERS * halves + h
        sq_send[h] = jnp.zeros((8, LANES), F32)
        wait_first(e)
        early[upper_half] = recv[e, upper_half]
        early[1 - upper_half, quarter(middle), :] = recv[e, 1 - upper_half, quarter(middle), :]
        early[1 - upper_half, quarter(1 - middle), :] = jnp.zeros((slots // 4, LANES), BF16)
        if 2 * wide > slots:
            early[1 - upper_half, slots // 2 :, :] = jnp.zeros((wide - slots // 2, LANES), BF16)

        @each_sub
        def _(s):
            left = term[h, span(s), :] - get_arrived(early, s)
            squares = left * left * weight[span(s), :]
            sq_send[h] = sq_send[h] + jnp.sum(squares.reshape(rows // 8, 8, LANES), axis=0)

        sq_recv[h, me] = sq_send[h]

        @pl.loop(0, parts)
        def _(i):
            each_peer(parts - 1 - i, lambda peer: sq_remote(h, peer).start())

        wait_rest(e)

        @each_sub
        def _(s):
            left = term[h, span(s), :] - get_arrived(recv.at[e], s)
            resid_out[s, :, lane(h)] = left * sign[span(s), :]

    @pl.loop(0, (ITERS + 1) * halves)
    def _(e):
        departure(e).wait_send()

    def sq_whole(h, wait_recv):
        copy = pltpu.make_async_remote_copy(
            src_ref=sq_recv.at[h, pl.ds(0, devices - 1)],
            dst_ref=sq_recv.at[h, pl.ds(0, devices - 1)],
            send_sem=sqs_sem.at[h],
            recv_sem=sqr_sem.at[h],
            device_id={"sub": flipped(me, 1, devices)},
            device_id_type=pl.DeviceIdType.MESH,
        )
        return copy.wait_recv() if wait_recv else copy.wait_send()

    for h in range(halves):
        sq_whole(h, False)
    for h in range(halves):
        sq_whole(h, True)
        everyone = jnp.sum(sq_recv[h], axis=0)
        everyone = jnp.sum(everyone, axis=0, keepdims=True)
        rms_out[:, h * LANES : (h + 1) * LANES] = jnp.sqrt(everyone / (count * devices) + 1e-06)


def store(mult, resid, rms, mult_out, resid_out, rms_out, sems):
    subs = mult.shape[0]
    copies = [pltpu.make_async_copy(rms, rms_out, sems.at[2 * subs])]
    for s in range(subs):
        copies.append(pltpu.make_async_copy(mult.at[s], mult_out.at[s], sems.at[2 * s]))
        copies.append(pltpu.make_async_copy(resid.at[s], resid_out.at[s], sems.at[2 * s + 1]))
    for copy in copies:
        copy.start()
    for copy in copies:
        copy.wait()


def local(factors, coupling, gap_loads, dof_blocks, partner_rows):
    subs, rows, cases = gap_loads.shape
    dof = factors.shape[1]
    devices = lax.axis_size("sub")
    count = subs * rows
    halves = cases // LANES
    spread = max(devices // 2 - 1, 1)
    capacity = FROWS * ((count // FROWS // 2 + spread - 1) // spread)
    slots = devices * capacity
    wide = -(-(slots // 2) // LANES) * LANES
    trips = (ITERS + 1) * halves
    vmem = pl.BlockSpec(memory_space=pltpu.VMEM)
    anywhere = pl.BlockSpec(memory_space=pltpu.HBM)
    mult, resid, rms = pl.pallas_call(
        functools.partial(kernel, devices, capacity),
        out_shape=(
            pltpu.VMEM((subs, rows, cases), F32),
            pltpu.VMEM((subs, rows, cases), F32),
            pltpu.VMEM((1, cases), F32),
        ),
        in_specs=[anywhere, anywhere, anywhere, anywhere, anywhere],
        out_specs=(vmem, vmem, vmem),
        scratch_shapes=[
            pltpu.VMEM((subs, rows, cases), BF16),
            pltpu.VMEM((subs, dof, dof), BF16),
            pltpu.VMEM((subs, dof, rows), BF16),
            pltpu.VMEM((slots, count // 2), BF16),
            pltpu.VMEM((slots, LANES), F32),
            pltpu.VMEM((count, wide), BF16),
            pltpu.VMEM((count, LANES), F32),
            pltpu.VMEM((subs, rows, rows), BF16),
            pltpu.VMEM((rows, dof), BF16),
            pltpu.VMEM((rows, dof), BF16),
            pltpu.VMEM((trips, slots, LANES), BF16),
            pltpu.VMEM((trips, 2, wide, LANES), BF16),
            pltpu.VMEM((halves, count // 2, 2 * LANES), BF16),
            pltpu.VMEM((halves, count, LANES), F32),
            pltpu.VMEM((halves, count, LANES), F32),
            pltpu.VMEM((count, LANES), F32),
            pltpu.VMEM((count, LANES), F32),
            pltpu.VMEM((2, wide, LANES), BF16),
            pltpu.VMEM((devices, count), F32),
            pltpu.VMEM((halves, 8, LANES), F32),
            pltpu.VMEM((halves, devices, 8, LANES), F32),
            pltpu.SemaphoreType.DMA,
            pltpu.SemaphoreType.DMA((subs,)),
            pltpu.SemaphoreType.DMA((subs,)),
            pltpu.SemaphoreType.DMA((trips,)),
            pltpu.SemaphoreType.DMA((trips, 3)),
            pltpu.SemaphoreType.DMA((halves,)),
            pltpu.SemaphoreType.DMA((halves,)),
            pltpu.SemaphoreType.REGULAR,
            pltpu.SemaphoreType.REGULAR,
            pltpu.VMEM((subs, rows), jnp.int32),
            pltpu.SemaphoreType.DMA,
            pltpu.SMEM((subs,), jnp.int32),
            pltpu.SemaphoreType.DMA,
        ],
        compiler_params=pltpu.CompilerParams(
            collective_id=0, has_side_effects=True, vmem_limit_bytes=58 * 1024 * 1024
        ),
    )(dof_blocks, factors, coupling, gap_loads, partner_rows)
    mult, resid, rms = (pltpu.with_memory_space_constraint(x, pltpu.VMEM) for x in (mult, resid, rms))
    mult, resid, rms = pl.pallas_call(
        store,
        out_shape=(
            jax.ShapeDtypeStruct((subs, rows, cases), F32),
            jax.ShapeDtypeStruct((subs, rows, cases), F32),
            jax.ShapeDtypeStruct((1, cases), F32),
        ),
        in_specs=[vmem, vmem, vmem],
        out_specs=(anywhere, anywhere, anywhere),
        scratch_shapes=[pltpu.SemaphoreType.DMA((2 * subs + 1,))],
        compiler_params=pltpu.CompilerParams(vmem_limit_bytes=1024 * 1024),
    )(mult, resid, rms)
    return mult, resid, rms.reshape(cases)


def solution(mesh):
    return jax.shard_map(
        local,
        mesh=mesh,
        in_specs=(
            P(("grp", "sub"), None, None),
            P(("grp", "sub"), None, None),
            P(("grp", "sub"), None, None),
            P(("grp", "sub")),
            P(("grp", "sub"), None),
        ),
        out_specs=(P(("grp", "sub"), None, None), P(("grp", "sub"), None, None), P("grp")),
        check_vma=False,
    )
```

```python
import functools

import jax
import jax.numpy as jnp
from jax import lax
from jax.experimental import pallas as pl
from jax.experimental.pallas import tpu as pltpu
from jax.sharding import PartitionSpec as P

DBLK = 128
FROWS = 16
ITERS = 3
STEP_SIZE = 0.25
LANES = 128
F32 = jnp.float32
BF16 = jnp.bfloat16


def flipped(me, distance, devices):
    peer = 0
    bit = 1
    while bit < devices:
        peer = peer + bit * ((me // bit + distance // bit) % 2)
        bit *= 2
    return peer


def kernel(
    devices, capacity, blocks_hbm, factors, coupling, gap_loads, partners_hbm,
    mult_out, resid_out, rms_out,
    gap, fac, cou, pack, pack_low, pick, pick_low, panel, turned, reduced, send, recv, low, term, mu, sign, weight, early,
    key, sq_send, sq_recv,
    gap_sem, fac_sem, cou_sem, send_sem, recv_sem, sqs_sem, sqr_sem, near_sem, far_sem, partners, partners_sem, blocks_ref, blocks_sem,
):
    subs, rows, cases = gap.shape
    dof = factors.shape[1]
    count = subs * rows
    halves = cases // LANES
    slots = devices * capacity
    wide = pick.shape[1]
    fold = count // 2
    band = rows // 2
    me = lax.axis_index("sub")
    parts = min(4, devices)
    group = devices // parts
    piece = slots // parts
    part = me // group
    inner = [flipped(me % group, d, group) for d in range(group)]

    middle = (part + 1) // 2 % 2
    outward = part + 1 - 2 * (part % 2)
    inward = parts - 1 - part
    upper_half = part // 2
    first_far = 3 - upper_half
    second_far = 2 + upper_half
    first_source = flipped(part, second_far, parts)

    def each_peer(far, action):
        side = flipped(part, far, parts)
        for d in range(group):
            peer = side * group + inner[d]
            if d > 0:
                action(peer)
            else:
                pl.when(far > 0)(functools.partial(action, peer))

    def fac_copy(s):
        return pltpu.make_async_copy(factors.at[s], fac.at[s], fac_sem.at[s])

    def cou_copy(s):
        return pltpu.make_async_copy(coupling.at[s], cou.at[s], cou_sem.at[s])

    gap_copy = pltpu.make_async_copy(gap_loads, gap, gap_sem)
    partners_copy = pltpu.make_async_copy(partners_hbm, partners, partners_sem)
    partners_copy.start()
    blocks_copy = pltpu.make_async_copy(blocks_hbm, blocks_ref, blocks_sem)
    blocks_copy.start()
    gap_copy.start()
    cou_copy(0).start(priority=1)
    fac_copy(0).start(priority=1)

    barrier = pltpu.get_barrier_semaphore()

    def greet(semaphore, peer):
        pl.semaphore_signal(
            semaphore, inc=1, device_id={"sub": peer}, device_id_type=pl.DeviceIdType.MESH
        )

    def greet_part(side):
        for d in range(group):
            greet(barrier, side * group + inner[d])

    pl.when(middle == 1)(lambda: greet_part(inward))
    greet_part(outward)
    for d in range(1, group):
        greet(barrier, part * group + inner[d])

    def place(i):
        at = pl.multiple_of(i % (devices // 2) * capacity, capacity)
        return i // (devices // 2), pl.ds(at, capacity)

    @pl.loop(0, recv.shape[0])
    def _(e):
        side, at = place(me)
        recv[e, side, at, :] = jnp.zeros((capacity, LANES), BF16)
        if 2 * wide > slots:
            for i in range(2):
                recv[e, i, slots // 2 :, :] = jnp.zeros((wide - slots // 2, LANES), BF16)

    partners_copy.wait()
    partner_row = jnp.concatenate([partners[s : s + 1, :] for s in range(subs)], axis=1).astype(F32)
    target_row = jnp.floor((partner_row + 0.5) * (1.0 / count))
    upper = (
        lax.broadcasted_iota(jnp.int32, (LANES, LANES), 0)
        <= lax.broadcasted_iota(jnp.int32, (LANES, LANES), 1)
    ).astype(F32).astype(BF16)
    peers = lax.broadcasted_iota(jnp.int32, (devices, LANES), 0).astype(F32)
    carry = jnp.zeros((devices, 1), F32)
    for b in range(count // LANES):
        hit = target_row[:, b * LANES : (b + 1) * LANES] == peers
        tally = jnp.dot(hit.astype(F32).astype(BF16), upper, preferred_element_type=F32) + carry
        key[:, b * LANES : (b + 1) * LANES] = jnp.where(hit, tally - 1.0, -1.0)
        carry = tally[:, LANES - 1 : LANES]

    slot_ids = lax.broadcasted_iota(jnp.int32, (capacity, count), 0).astype(F32)

    def build(side):
        @pl.loop(side * group, (side + 1) * group)
        def _(p):
            chosen = jnp.where(key[pl.ds(p, 1), :] == slot_ids, 1.0, 0.0)
            at = pl.ds(pl.multiple_of(p * capacity, capacity), capacity)
            lower = chosen[:, :fold]
            pack[at, :] = (lower + chosen[:, fold:]).astype(BF16)
            pack_low[at, :] = jnp.broadcast_to(jnp.sum(lower, axis=1, keepdims=True), (capacity, LANES))

    def chunk(i):
        return pl.ds(pl.multiple_of(i * capacity, capacity), capacity)

    def remote(e, peer, crossing):
        return pltpu.make_async_remote_copy(
            src_ref=send.at[e, chunk(peer)],
            dst_ref=recv.at[e, *place(me)],
            send_sem=send_sem.at[e],
            recv_sem=recv_sem.at[e, crossing],
            device_id={"sub": peer},
            device_id_type=pl.DeviceIdType.MESH,
        )

    def arrival(e, crossing, chunks):
        at = pl.ds(0, chunks * capacity)
        return pltpu.make_async_remote_copy(
            src_ref=recv.at[e, 0, at],
            dst_ref=recv.at[e, 0, at],
            send_sem=send_sem.at[e],
            recv_sem=recv_sem.at[e, crossing],
            device_id={"sub": flipped(me, 1, devices)},
            device_id_type=pl.DeviceIdType.MESH,
        )

    def departure(e):
        at = pl.ds(0, (devices - 1) * capacity)
        return pltpu.make_async_remote_copy(
            src_ref=send.at[e, at],
            dst_ref=send.at[e, at],
            send_sem=send_sem.at[e],
            recv_sem=recv_sem.at[e, 0],
            device_id={"sub": flipped(me, 1, devices)},
            device_id_type=pl.DeviceIdType.MESH,
        )

    def either(lower, pair):
        return jnp.where(lower > 0.5, pair[:, :LANES], pair[:, LANES:])

    def fill(e, h, side):
        at = pl.ds(pl.multiple_of(side * piece, piece), piece)
        pair = jnp.dot(pack[at, :], low[h], preferred_element_type=F32)
        send[e, at, :] = either(pack_low[at, :], pair).astype(BF16)

    def post(e, far):
        crossing = jnp.where(far < parts // 2, 0, jnp.where(far == first_far, 1, 2))
        each_peer(far, lambda peer: remote(e, peer, crossing).start())

    def wait_first(e):
        arrival(e, 0, devices // 2 - 1).wait_recv()
        arrival(e, 1, group).wait_recv()

    def wait_rest(e):
        arrival(e, 2, group).wait_recv()

    def lane(h):
        return pl.ds(pl.multiple_of(h * LANES, LANES), LANES)

    def span(s):
        return pl.ds(pl.multiple_of(s * rows, rows), rows)

    def quarter(i):
        return pl.ds(pl.multiple_of(i * (slots // 4), capacity), slots // 4)

    def each_sub(body):
        for s in range(subs):
            body(s)

    def each_part(body):
        for i in range(parts):
            body(i)

    def set_low(h, s, values):
        for i in range(2):
            q = 2 * s + i
            at = pl.ds(pl.multiple_of(q % subs * band, band), band)
            low[h, at, lane(q // subs)] = values[i * band : (i + 1) * band, :]

    def get_arrived(source, s):
        both = jnp.concatenate([source[0], source[1]], axis=1)
        pair = jnp.dot(pick[span(s), :], both, preferred_element_type=F32)
        return either(pick_low[span(s), :], pair)

    gap_copy.wait()
    for h in range(halves):
        for s in range(subs):
            values = gap[s, :, h * LANES : (h + 1) * LANES]
            set_low(h, s, values)
    def turn(i):
        return middle * (parts - 1 - i) + (1 - middle) * ((i + 1) % parts)

    build(flipped(part, turn(0), parts))
    pl.semaphore_wait(barrier, (2 + middle) * group - 1)

    @pl.when(middle == 1)
    def _():
        greet(near_sem, inward * group + inner[0])
        greet(near_sem, outward * group + inner[0])

    def begin(h, i):
        fill(h, h, flipped(part, turn(i), parts))
        post(h, turn(i))

    @pl.loop(0, parts * halves)
    def _(t):
        first = t // halves == 0
        u = jnp.maximum(t - halves, 0)
        h = jnp.where(first, t, u // (parts - 1))
        i = jnp.where(first, 0, u % (parts - 1) + 1)

        @pl.when((t >= halves) & (h == 0))
        def _():
            build(flipped(part, turn(i), parts))

        @pl.when(t == halves)
        def _():
            pl.semaphore_wait(near_sem, 1)
            pl.when(middle == 1)(lambda: greet(far_sem, outward * group + inner[0]))

        @pl.when((t == halves + 1) & (middle == 0))
        def _():
            pl.semaphore_wait(far_sem, 1)

        begin(h, i)

    for h in range(halves):
        for s in range(subs):
            term[h, s * rows : (s + 1) * rows, :] = gap[s, :, h * LANES : (h + 1) * LANES].astype(F32)
    mu[...] = jnp.zeros_like(mu)

    bands = rows // LANES
    tile = dof // bands
    lanes = lax.broadcasted_iota(jnp.int32, (LANES, LANES), 1).astype(F32)
    sublanes = lax.broadcasted_iota(jnp.int32, (LANES, LANES), 0)

    def find(s, j):
        base = s * rows + j * LANES
        at = pl.ds(pl.multiple_of(base, LANES), LANES)
        mine = partners[pl.ds(s, 1), pl.ds(pl.multiple_of(j * LANES, LANES), LANES)].astype(F32)
        across = jnp.transpose(jnp.broadcast_to(mine, (LANES, LANES)))
        target = jnp.floor((across + 0.5) * (1.0 / count))
        first = target * count
        tally = jnp.zeros((LANES, LANES), F32)
        for c in range(count // LANES):
            other = partner_row[:, c * LANES : (c + 1) * LANES]
            tally = tally + jnp.where((other < across) & (other >= first), 1.0, 0.0)
        slot = target * capacity + jnp.sum(tally, axis=1, keepdims=True)
        own = (sublanes + (me * count + base)).astype(F32)
        sign[at, :] = jnp.where(own < across, 1.0, -1.0)
        low_near = (upper_half * (devices // 2)).astype(F32)
        near = (target >= low_near) & (target < low_near + devices // 2)
        low_first = (first_source * group).astype(F32)
        soon = (target >= low_first) & (target < low_first + group)
        weight[at, :] = jnp.where(near, 1.0, jnp.where(soon, 2.0, 0.0))
        half = slots // 2
        lower = slot < half
        slot = jnp.where(lower, slot, slot - half)
        pick_low[at, :] = jnp.broadcast_to(jnp.where(lower, 1.0, 0.0), (LANES, LANES))
        for c in range(wide // LANES):
            pick[at, c * LANES : (c + 1) * LANES] = jnp.where(
                slot - c * LANES == lanes, 1.0, 0.0
            ).astype(BF16)

    blocks_copy.wait()
    for s in range(subs):
        cou_copy(s).wait()
        fac_copy(s).wait()
        if s + 1 < subs:
            cou_copy(s + 1).start(priority=1)
            fac_copy(s + 1).start(priority=1)
        limit = blocks_ref[s] * DBLK
        present = lax.broadcasted_iota(jnp.int32, (dof, rows), 0) < limit
        turned[...] = jnp.transpose(jnp.where(present, cou[s], jnp.zeros((dof, rows), BF16)))

        @pl.loop(0, bands)
        def _(j):
            at = pl.ds(pl.multiple_of(j * tile, tile), tile)
            product = jnp.dot(turned[...], fac[s, :, at], preferred_element_type=F32)
            find(s, j)
            keep = lax.broadcasted_iota(jnp.int32, (rows, tile), 1) + j * tile < limit
            reduced[:, at] = jnp.where(keep, product, 0.0).astype(BF16)

        panel[s] = lax.dot_general(
            reduced[...], reduced[...], (((1,), (1,)), ((), ())), preferred_element_type=F32
        ).astype(BF16)

    @pl.loop(0, ITERS * halves)
    def _(e):
        h = e % halves
        wait_first(e)
        wait_rest(e)

        @each_sub
        def _(s):
            at = span(s)
            arrived = get_arrived(recv.at[e], s)
            moved = mu[h, at, :] + STEP_SIZE * (term[h, at, :] - arrived)
            mu[h, at, :] = moved
            image = jnp.dot(panel[s], moved.astype(BF16), preferred_element_type=F32)
            left = gap[s, :, lane(h)].astype(F32) - image
            term[h, at, :] = left
            set_low(h, s, left.astype(BF16))

        @each_part
        def _(i):
            far = jnp.where(e < (ITERS - 1) * halves, parts - 1 - i, (1, 0, first_far, second_far)[i])
            fill(e + halves, h, flipped(part, far, parts))
            post(e + halves, far)

    @pl.loop(0, halves)
    def _(h):
        @pl.loop(0, subs)
        def _(s):
            mult_out[s, :, lane(h)] = mu[h, span(s), :] * sign[span(s), :]

    def sq_remote(h, peer):
        return pltpu.make_async_remote_copy(
            src_ref=sq_send.at[h],
            dst_ref=sq_recv.at[h, me],
            send_sem=sqs_sem.at[h],
            recv_sem=sqr_sem.at[h],
            device_id={"sub": peer},
            device_id_type=pl.DeviceIdType.MESH,
        )

    @pl.loop(0, halves)
    def _(h):
        e = ITERS * halves + h
        sq_send[h] = jnp.zeros((8, LANES), F32)
        wait_first(e)
        early[upper_half] = recv[e, upper_half]
        early[1 - upper_half, quarter(middle), :] = recv[e, 1 - upper_half, quarter(middle), :]
        early[1 - upper_half, quarter(1 - middle), :] = jnp.zeros((slots // 4, LANES), BF16)
        if 2 * wide > slots:
            early[1 - upper_half, slots // 2 :, :] = jnp.zeros((wide - slots // 2, LANES), BF16)

        @each_sub
        def _(s):
            left = term[h, span(s), :] - get_arrived(early, s)
            squares = left * left * weight[span(s), :]
            sq_send[h] = sq_send[h] + jnp.sum(squares.reshape(rows // 8, 8, LANES), axis=0)

        sq_recv[h, me] = sq_send[h]

        @pl.loop(0, parts)
        def _(i):
            each_peer(parts - 1 - i, lambda peer: sq_remote(h, peer).start())

        wait_rest(e)

        @each_sub
        def _(s):
            left = term[h, span(s), :] - get_arrived(recv.at[e], s)
            resid_out[s, :, lane(h)] = left * sign[span(s), :]

    @pl.loop(0, (ITERS + 1) * halves)
    def _(e):
        departure(e).wait_send()

    def sq_whole(h, wait_recv):
        copy = pltpu.make_async_remote_copy(
            src_ref=sq_recv.at[h, pl.ds(0, devices - 1)],
            dst_ref=sq_recv.at[h, pl.ds(0, devices - 1)],
            send_sem=sqs_sem.at[h],
            recv_sem=sqr_sem.at[h],
            device_id={"sub": flipped(me, 1, devices)},
            device_id_type=pl.DeviceIdType.MESH,
        )
        return copy.wait_recv() if wait_recv else copy.wait_send()

    for h in range(halves):
        sq_whole(h, False)
    for h in range(halves):
        sq_whole(h, True)
        everyone = jnp.sum(sq_recv[h], axis=0)
        everyone = jnp.sum(everyone, axis=0, keepdims=True)
        rms_out[:, h * LANES : (h + 1) * LANES] = jnp.sqrt(everyone / (count * devices) + 1e-06)


def store(mult, resid, rms, mult_out, resid_out, rms_out, sems):
    subs = mult.shape[0]
    copies = [pltpu.make_async_copy(rms, rms_out, sems.at[2 * subs])]
    for s in range(subs):
        copies.append(pltpu.make_async_copy(mult.at[s], mult_out.at[s], sems.at[2 * s]))
        copies.append(pltpu.make_async_copy(resid.at[s], resid_out.at[s], sems.at[2 * s + 1]))
    for copy in copies:
        copy.start()
    for copy in copies:
        copy.wait()


def local(factors, coupling, gap_loads, dof_blocks, partner_rows):
    subs, rows, cases = gap_loads.shape
    dof = factors.shape[1]
    devices = lax.axis_size("sub")
    count = subs * rows
    halves = cases // LANES
    spread = max(devices // 2 - 1, 1)
    capacity = FROWS * ((count // FROWS // 2 + spread - 1) // spread)
    slots = devices * capacity
    wide = -(-(slots // 2) // LANES) * LANES
    trips = (ITERS + 1) * halves
    vmem = pl.BlockSpec(memory_space=pltpu.VMEM)
    anywhere = pl.BlockSpec(memory_space=pltpu.HBM)
    mult, resid, rms = pl.pallas_call(
        functools.partial(kernel, devices, capacity),
        out_shape=(
            pltpu.VMEM((subs, rows, cases), F32),
            pltpu.VMEM((subs, rows, cases), F32),
            pltpu.VMEM((1, cases), F32),
        ),
        in_specs=[anywhere, anywhere, anywhere, anywhere, anywhere],
        out_specs=(vmem, vmem, vmem),
        scratch_shapes=[
            pltpu.VMEM((subs, rows, cases), BF16),
            pltpu.VMEM((subs, dof, dof), BF16),
            pltpu.VMEM((subs, dof, rows), BF16),
            pltpu.VMEM((slots, count // 2), BF16),
            pltpu.VMEM((slots, LANES), F32),
            pltpu.VMEM((count, wide), BF16),
            pltpu.VMEM((count, LANES), F32),
            pltpu.VMEM((subs, rows, rows), BF16),
            pltpu.VMEM((rows, dof), BF16),
            pltpu.VMEM((rows, dof), BF16),
            pltpu.VMEM((trips, slots, LANES), BF16),
            pltpu.VMEM((trips, 2, wide, LANES), BF16),
            pltpu.VMEM((halves, count // 2, 2 * LANES), BF16),
            pltpu.VMEM((halves, count, LANES), F32),
            pltpu.VMEM((halves, count, LANES), F32),
            pltpu.VMEM((count, LANES), F32),
            pltpu.VMEM((count, LANES), F32),
            pltpu.VMEM((2, wide, LANES), BF16),
            pltpu.VMEM((devices, count), F32),
            pltpu.VMEM((halves, 8, LANES), F32),
            pltpu.VMEM((halves, devices, 8, LANES), F32),
            pltpu.SemaphoreType.DMA,
            pltpu.SemaphoreType.DMA((subs,)),
            pltpu.SemaphoreType.DMA((subs,)),
            pltpu.SemaphoreType.DMA((trips,)),
            pltpu.SemaphoreType.DMA((trips, 3)),
            pltpu.SemaphoreType.DMA((halves,)),
            pltpu.SemaphoreType.DMA((halves,)),
            pltpu.SemaphoreType.REGULAR,
            pltpu.SemaphoreType.REGULAR,
            pltpu.VMEM((subs, rows), jnp.int32),
            pltpu.SemaphoreType.DMA,
            pltpu.SMEM((subs,), jnp.int32),
            pltpu.SemaphoreType.DMA,
        ],
        compiler_params=pltpu.CompilerParams(
            collective_id=0, has_side_effects=True, vmem_limit_bytes=58 * 1024 * 1024
        ),
    )(dof_blocks, factors, coupling, gap_loads, partner_rows)
    mult, resid, rms = (pltpu.with_memory_space_constraint(x, pltpu.VMEM) for x in (mult, resid, rms))
    mult, resid, rms = pl.pallas_call(
        store,
        out_shape=(
            jax.ShapeDtypeStruct((subs, rows, cases), F32),
            jax.ShapeDtypeStruct((subs, rows, cases), F32),
            jax.ShapeDtypeStruct((1, cases), F32),
        ),
        in_specs=[vmem, vmem, vmem],
        out_specs=(anywhere, anywhere, anywhere),
        scratch_shapes=[pltpu.SemaphoreType.DMA((2 * subs + 1,))],
        compiler_params=pltpu.CompilerParams(vmem_limit_bytes=1024 * 1024),
    )(mult, resid, rms)
    return mult, resid, rms.reshape(cases)


def solution(mesh):
    return jax.shard_map(
        local,
        mesh=mesh,
        in_specs=(
            P(("grp", "sub"), None, None),
            P(("grp", "sub"), None, None),
            P(("grp", "sub"), None, None),
            P(("grp", "sub")),
            P(("grp", "sub"), None),
        ),
        out_specs=(P(("grp", "sub"), None, None), P(("grp", "sub"), None, None), P("grp")),
        check_vma=False,
    )
```
